256 devices in a mesh: seq: 16 (over z, core), mp: 16 (over x, y).
Axes of the slice: x: 4, y: 4, z: 8, core: 2. Of those that a mesh axis runs over, the one named last changes fastest.
Arguments:
- fine_rows: bfloat16 [49152, 4096], P(('seq', 'mp')), may hold values from -6 to 6
- w_inputs: bfloat16 [4096, 4, 4096], P(None, None, 'mp'), may hold values from -0.375 to 0.375
- w_out: bfloat16 [4096, 4096], P('mp'), may hold values from -0.09375 to 0.09375
- head_gain: float32 [4096], P('mp'), may hold values from 0.1 to 1.9
- decay_log: float32 [32, 12288], P('mp', 'seq'), may hold values from -1 to 0, as said below
Outputs:
- fine_output: bfloat16 [49152, 4096], P(('seq', 'mp'))
The draws below stay inside these ranges and needn't reach their ends.
Inputs may be any that keep to these rules, and one draw needn't show every extreme that they name: `decay_log`: entries are logarithms of decay factors, one for each head and coarse row.
All inputs are finite; a program needn't handle non-finite values.
Results may differ from the reference program's by a relative error of at most 0.018.
Values may be sent and summed in bfloat16 or wider, within the bound.
A program may use at most 128 MiB of HBM per device.

```python
import math
import jax
import jax.numpy as jnp
from jax import lax

D = 4096
ATTENDER_NUMBER = 32
SF = 4
CH = 128
LC_DEV = 768
HEADS_DEV = 2
POOLED_SPAN = 12288
LF = 49152
N_MP = 16


def draw_decay_log(key, part):
    fast_share = 0.5
    kind_draw = jax.random.uniform(jax.random.fold_in(key, 1), (ATTENDER_NUMBER, 1))
    fast_rate = 1.0 / jnp.exp(jax.random.uniform(jax.random.fold_in(key, 2), (ATTENDER_NUMBER, 1), minval=math.log(30.0), maxval=math.log(50.0)))
    slow_rate = jnp.exp(jax.random.uniform(jax.random.fold_in(key, 3), (ATTENDER_NUMBER, 1), minval=math.log(0.3), maxval=math.log(0.8))) / POOLED_SPAN
    reference_speed = jnp.where(kind_draw < fast_share, fast_rate, slow_rate)
    shard_count = POOLED_SPAN // LC_DEV
    portion_scaling_factor = jnp.exp(jax.random.uniform(jax.random.fold_in(key, 4), (ATTENDER_NUMBER, shard_count, 1), minval=math.log(0.6), maxval=math.log(1.6)))
    portion_scaling_factor = jnp.broadcast_to(portion_scaling_factor, (ATTENDER_NUMBER, shard_count, LC_DEV)).reshape(ATTENDER_NUMBER, POOLED_SPAN)
    entry_scaling_factor = jax.random.uniform(jax.random.fold_in(key, 5), (ATTENDER_NUMBER, POOLED_SPAN), minval=0.5, maxval=1.5)
    spell_chosen = jax.random.uniform(jax.random.fold_in(key, 6), (ATTENDER_NUMBER, POOLED_SPAN))
    spell_extent = jnp.log(jax.random.uniform(jax.random.fold_in(key, 7), (ATTENDER_NUMBER, POOLED_SPAN), minval=0.5, maxval=0.8))
    spell_sequence_items = jnp.where(spell_chosen < 2.0 / POOLED_SPAN, spell_extent, 0.0)
    return (-reference_speed * portion_scaling_factor * entry_scaling_factor + spell_sequence_items).astype(jnp.float32)


def block_levels(own_key, extent, pieces, least, high):
    factor_of, own = 1.0, jax.random.fold_in(own_key, 6)
    for axis_at, shards_of in pieces:
        steps = jnp.exp(jax.random.uniform(jax.random.fold_in(own, axis_at), (shards_of,), jnp.float32, least / len(pieces), high / len(pieces)))
        factor_of = factor_of * jnp.repeat(steps, extent[axis_at] // shards_of).reshape([-1 if axis == axis_at else 1 for axis in range(len(extent))])
    return factor_of


def scatter_about(stream_key, extent, width, limit, cuts=(), held_as=jnp.bfloat16):
    array = width * jax.random.normal(stream_key, extent, jnp.float32)
    if cuts:
        array = array * block_levels(stream_key, extent, cuts, -0.22, 0.18)
    return jnp.clip(array, -limit, limit).astype(held_as)


def setup_inputs(seed: int = 0) -> dict:
    arg_keys = jax.random.split(jax.random.key(seed), 6)
    return {
        "fine_rows": scatter_about(arg_keys[0], (LF, D), 1.0, 6.0, ((0, 256),)),
        "w_inputs": scatter_about(arg_keys[1], (D, 4, D), (D // 16) ** -0.5, 0.375, ((2, 16),)),
        "w_out": scatter_about(arg_keys[2], (D, D), D ** -0.5, 0.09375, ((0, 16),)),
        "head_gain": jnp.clip(1.0 + 0.18 * jax.random.normal(arg_keys[3], (D,), jnp.float32), 0.1, 1.9),
        "decay_log": draw_decay_log(jax.random.fold_in(arg_keys[5], 71), 0),
    }


EPSILON = 1e-05

def reference(fine_rows, w_inputs, w_out, head_gain, decay_log):
    head_dim = D // ATTENDER_NUMBER
    blocks = POOLED_SPAN // CH
    widened = jnp.concatenate([jnp.zeros((SF - 1, D), jnp.float32), fine_rows[:LF - (SF - 1)].astype(jnp.float32)], axis=0)
    pooled = lax.optimization_barrier(jnp.mean(widened.reshape(POOLED_SPAN, SF, D), axis=1)).astype(jnp.bfloat16)

    def project(slot_number):
        return jnp.dot(pooled, w_inputs[:, slot_number, :], preferred_element_type=jnp.float32)
    queries = project(0).astype(jnp.bfloat16).reshape(blocks, CH, ATTENDER_NUMBER, head_dim)
    key_rows = project(1).astype(jnp.bfloat16).reshape(blocks, CH, ATTENDER_NUMBER, head_dim)
    values = project(2).astype(jnp.bfloat16).reshape(blocks, CH, ATTENDER_NUMBER, head_dim)
    gate_values = project(3)
    decays = decay_log.reshape(ATTENDER_NUMBER, blocks, CH).transpose(1, 0, 2)
    causal = jnp.arange(CH)[:, None] >= jnp.arange(CH)[None, :]

    def advance(state, inputs):
        query_block, key_block, value_block, decay_block = inputs
        cumulative = jnp.cumsum(decay_block, axis=1)
        gaps = cumulative[:, :, None] - cumulative[:, None, :]
        weight = jnp.where(causal, jnp.exp(jnp.minimum(gaps, 0.0)), 0.0)
        scores = jnp.einsum('thd,shd->hts', query_block.astype(jnp.float32), key_block.astype(jnp.float32)) * weight
        scores = lax.optimization_barrier(scores.astype(jnp.bfloat16)).astype(jnp.float32)
        within = jnp.einsum('hts,shd->thd', scores, value_block.astype(jnp.float32))
        rounded = lax.optimization_barrier(state.astype(jnp.bfloat16)).astype(jnp.float32)
        summed = jnp.einsum('thd,hde->the', query_block.astype(jnp.float32), rounded) * jnp.exp(cumulative).T[:, :, None]
        remaining = jnp.exp(cumulative[:, -1:] - cumulative)
        decayed = (key_block.astype(jnp.float32) * remaining.T[:, :, None]).astype(jnp.bfloat16)
        decayed = lax.optimization_barrier(decayed).astype(jnp.float32)
        new_state = jnp.exp(cumulative[:, -1])[:, None, None] * state + jnp.einsum('shd,she->hde', decayed, value_block.astype(jnp.float32))
        return (new_state, within + summed)
    initial = jnp.zeros((ATTENDER_NUMBER, head_dim, head_dim), jnp.float32)
    _, attended = lax.scan(advance, initial, (queries, key_rows, values, decays))
    attended = attended.reshape(POOLED_SPAN, ATTENDER_NUMBER, head_dim)
    square_mean = lax.optimization_barrier(jnp.mean(attended * attended, axis=2, keepdims=True))
    normed = (attended * lax.rsqrt(square_mean + EPSILON)).reshape(POOLED_SPAN, D)
    gated_rows = (normed * head_gain * jax.nn.silu(gate_values)).astype(jnp.bfloat16)
    group_width = HEADS_DEV * head_dim
    coarse = jnp.zeros((POOLED_SPAN, D), jnp.float32)
    for group_index in range(N_MP):
        group_term = jnp.dot(gated_rows[:, group_index * group_width:(group_index + 1) * group_width], w_out[group_index * group_width:(group_index + 1) * group_width], preferred_element_type=jnp.float32)
        coarse = coarse + lax.optimization_barrier(group_term.astype(jnp.bfloat16)).astype(jnp.float32)
    return (fine_rows.astype(jnp.float32) + jnp.repeat(coarse, SF, axis=0)).astype(jnp.bfloat16)
```

```python
import functools

import jax
import jax.numpy as jnp
from jax import lax
from jax.experimental import pallas as pl
from jax.experimental.pallas import tpu as pltpu
from jax.sharding import PartitionSpec as P

BF = jnp.bfloat16
F32 = jnp.float32
MESH = pl.DeviceIdType.MESH
EPSILON = 1e-05
CW = 512
NC = 8
NZ = 8


def dot(a, b):
    return jnp.dot(a, b, preferred_element_type=F32)


def main_kernel(
    fine, w, wo_hbm, gain, decay, out,
    fine_v, rows_f, tail_s, tail_r, g, w_raw, w_f, w_v, acc, wg, wo,
    gated2, gated, ha, ps, pr,
    wgt, ecum, rem, cend, bsv, run, s_s, s_r, c_s, c_r, i_s, i_r, inc, within, d_o, d_s,
    l_fine, l_w, l_wo,
    tail_sem, p1s, p1r, p2s, p2r, w0s, w0r, rgs, rgr, sbs, sbr,
    dds, ddr, dss, ss, cs_s, cs_r, is_s, as_s, as_r, rs_s, rs_r,
):
    sq, mp = lax.axis_index("seq"), lax.axis_index("mp")
    z, c = lax.div(sq, 2), lax.rem(sq, 2)
    x, y = lax.div(mp, 4), lax.rem(mp, 4)
    flat = sq * 16 + mp

    def at_x(d):
        return (sq, lax.rem(x + d, 4) * 4 + y)

    def at_y(d):
        return (sq, x * 4 + lax.rem(y + d, 4))

    def at_z(d):
        return (lax.rem(z + d, NZ) * 2 + c, mp)

    sibling = (z * 2 + 1 - c, mp)
    after, before = lax.rem(flat + 1, 256), lax.rem(flat + 255, 256)
    after = (lax.div(after, 16), lax.rem(after, 16))
    before = (lax.div(before, 16), lax.rem(before, 16))

    def rc(src, dst, send, recv, dev):
        return pltpu.make_async_remote_copy(
            src_ref=src, dst_ref=dst, send_sem=send, recv_sem=recv,
            device_id=dev, device_id_type=MESH,
        )

    barrier = pltpu.get_barrier_semaphore()
    partners = (
        [at_x(d) for d in (1, 2, 3)] + [at_y(d) for d in (1, 2, 3)]
        + [at_z(d) for d in range(1, NZ)] + [sibling, after, before]
    )
    for dev in partners:
        pl.semaphore_signal(barrier, inc=1, device_id=dev, device_id_type=MESH)

    fine_in = [
        pltpu.make_async_copy(fine.at[:, i * CW:(i + 1) * CW], fine_v.at[i], l_fine.at[i])
        for i in range(NC)
    ]
    for copy in fine_in:
        copy.start()

    def w_in(i, slot):
        return pltpu.make_async_copy(
            w.at[pl.ds(pl.multiple_of(i * CW * 8, CW * 8), CW * 8), :], w_raw.at[slot], l_w.at[slot]
        )

    w_in(0, 0).start()
    w_in(1, 1).start()
    wo_in = pltpu.make_async_copy(wo_hbm, wo, l_wo)
    wo_in.start()

    for copy in fine_in:
        copy.wait()

    def pool_into(i, first, count):
        for q in range(4):
            total = rows_f[4 * i + q, pl.ds(5 + 4 * first, count, stride=4), :]
            for m in (1, 2, 3):
                total += rows_f[4 * i + q, pl.ds(5 + 4 * first + m, count, stride=4), :]
            g[i, x, y, first:first + count, q * 128:(q + 1) * 128] = (total * 0.25).astype(BF)

    @pl.loop(0, NC)
    def _(i):
        for q in range(4):
            cols = slice(q * 128, (q + 1) * 128)
            rows_f[4 * i + q, 8:200, :] = fine_v[i, :, cols].astype(F32)
            tail_s[i, :, cols] = rows_f[4 * i + q, 192:200, :].astype(BF)
        pool_into(i, 16, 32)

    total = jnp.sum(decay[...], axis=1, keepdims=True)
    d_o[0] = jnp.zeros((8, 128), F32)
    d_o[0, 0:2, :] = jnp.broadcast_to(total, (2, 128))

    pl.semaphore_wait(barrier, len(partners))

    tail = rc(tail_s, tail_r, tail_sem.at[0], tail_sem.at[1], after)
    tail.start()

    def d_copy(d):
        return rc(d_o.at[0], d_o.at[d], dds.at[d - 1], ddr.at[d - 1], at_z(d))

    for d in range(1, NZ):
        d_copy(d).start()

    mine = pl.ds(pl.multiple_of(sq * 16, 16), 16)

    def w0(kind, d):
        j = kind * 3 + 3 - d
        return rc(
            wo_hbm.at[mine, kind * 2048:(kind + 1) * 2048], wg.at[j, mine, :],
            w0s.at[j], w0r.at[j], at_x(d) if kind == 0 else at_y(d),
        )

    acc[...] = jnp.zeros_like(acc)

    def first(i, kind, d):
        block = g.at[i, x, y]
        k = 0 if d == 1 else 1
        return rc(block, block, p1s.at[i, k], p1r.at[i, k], (at_x if kind == 0 else at_y)(d))

    def first_pass(i, kind, d):
        cols = pl.ds(0, 256) if d == 1 else pl.ds(256, 256)
        from_x = lax.rem(x + (4 - d), 4) if kind == 0 else x
        from_y = y if kind == 0 else lax.rem(y + (4 - d), 4)
        block = g.at[i, from_x, from_y, :, cols]
        k = 2 if d == 1 else 3
        return rc(block, block, p1s.at[i, k], p1r.at[i, k], (at_x if kind == 0 else at_y)(d))

    def second(i, kind, d):
        block = g.at[i, :, y] if kind == 0 else g.at[i, x]
        k = 0 if d == 1 else 1
        return rc(block, block, p2s.at[i, k], p2r.at[i, k], (at_y if kind == 0 else at_x)(d))

    def second_pass(i, kind, d):
        cols = pl.ds(0, 256) if d == 1 else pl.ds(256, 256)
        if kind == 0:
            block = g.at[i, :, lax.rem(y + (4 - d), 4), :, cols]
        else:
            block = g.at[i, lax.rem(x + (4 - d), 4), :, :, cols]
        k = 2 if d == 1 else 3
        return rc(block, block, p2s.at[i, k], p2r.at[i, k], (at_y if kind == 0 else at_x)(d))

    def both(make, p, act):
        for kind in (0, 1):
            for d in (1, 3):
                getattr(make(2 * p + kind, kind, d), act)()

    tail.wait_recv()
    is_first = flat == 0

    @pl.loop(0, 4)
    def _(p):
        for kind in (0, 1):
            i = 2 * p + kind
            for q in range(4):
                rows_f[4 * i + q, 0:8, :] = jnp.where(
                    is_first, 0.0, tail_r[i, :, q * 128:(q + 1) * 128].astype(F32)
                )
            pool_into(i, 0, 16)
        both(first, p, "start")

    for kind in (0, 1):
        for d in (1, 2, 3):
            w0(kind, d).start()

    def relayout(i, slot):
        w_in(i, slot).wait()
        w_f[...] = w_raw[slot].astype(F32)
        for s in range(4):
            for h in range(2):
                w_v[i, :, s * 256 + h * 128:s * 256 + (h + 1) * 128] = w_f[
                    pl.ds(h * 4 + s, CW, stride=8), :
                ].astype(BF)

        @pl.when(i + 2 < NC)
        def _():
            w_in(i + 2, slot).start()

    @pl.loop(0, 4)
    def _(p):
        relayout(2 * p, 0)
        both(first, p, "wait_recv")
        both(first_pass, p, "start")
        relayout(2 * p + 1, 1)

    def rows_of(zz, cc):
        return pl.ds(pl.multiple_of((lax.rem(zz, NZ) * 2 + cc) * 16, 16), 16)

    def ring(k, right):
        which = slice(0, 6) if k < 4 else (slice(0, 3) if right else slice(3, 6))
        rows = rows_of(z + (NZ - (k - 1)) if right else z + (k - 1), c)
        block = wg.at[which, rows, :]
        n = 2 * (k - 1) + (0 if right else 1)
        return rc(block, block, rgs.at[n], rgr.at[n], at_z(1 if right else NZ - 1))

    def share(n):
        zz = z + (0, NZ - 1, NZ - 2, NZ - 3, 1, 2, 3, 4)[n]
        block = wg.at[:, rows_of(zz, c), :]
        return rc(block, block, sbs.at[n], sbr.at[n], sibling)

    def share_wait(n):
        zz = z + (0, NZ - 1, NZ - 2, NZ - 3, 1, 2, 3, 4)[n]
        block = wg.at[:, rows_of(zz, 1 - c), :]
        rc(block, block, sbs.at[n], sbr.at[n], sibling).wait_recv()

    def ring_step(k):
        ring(k, True).wait_recv()
        ring(k, False).wait_recv()
        if k < 4:
            ring(k + 1, True).start()
            ring(k + 1, False).start()
            share(k).start()
            share(3 + k).start()
        else:
            share(7).start()

    @pl.loop(0, 4)
    def _(p):
        both(first_pass, p, "wait_recv")

        @pl.when(p < 2)
        def _():
            both(second, p, "start")

    for kind in (0, 1):
        for d in (1, 2, 3):
            w0(kind, d).wait_recv()
    ring(1, True).start()
    ring(1, False).start()
    share(0).start()

    for d in range(1, NZ):
        d_copy(d).wait_recv()
    d_share = rc(d_o, d_s, dss.at[0], dss.at[1], sibling)
    d_share.start()

    t_i = lax.broadcasted_iota(jnp.int32, (128, 128), 0)
    s_i = lax.broadcasted_iota(jnp.int32, (128, 128), 1)
    causal = t_i >= s_i
    lower = jnp.where(causal, 1.0, 0.0).astype(F32)
    nt = (((1,), (1,)), ((), ()))
    tn = (((0,), (0,)), ((), ()))
    for b in range(6):
        for h in range(2):
            rep = jnp.broadcast_to(decay[h:h + 1, b * 128:(b + 1) * 128], (128, 128))
            col = lax.dot_general(lower, rep, nt, precision=lax.Precision.HIGHEST, preferred_element_type=F32)
            row = lax.dot_general(rep, lower, nt, precision=lax.Precision.HIGHEST, preferred_element_type=F32)
            wgt[b, h] = jnp.where(causal, jnp.exp(jnp.minimum(col - row, 0.0)), 0.0)
            ecum[b, h] = jnp.exp(col)
            end = col[127:128, :]
            rem[b, h] = jnp.exp(end - col)
            cend[b, h] = jnp.broadcast_to(jnp.exp(end), (8, 128))

    def project(p):
        both(second_pass, p, "wait_recv")

        @pl.loop(0, 8)
        def _(t):
            i2 = lax.div(t, 4)
            n = lax.rem(t, 4)
            rows = pl.ds(pl.multiple_of(i2 * 384, 384), 384)
            cols = pl.ds(pl.multiple_of(n * 256, 256), 256)
            part = acc[rows, cols]
            for kind in (0, 1):
                i = 2 * p + kind
                left = g[i, pl.ds(i2 * 2, 2)].reshape(384, CW)
                part += dot(left, w_v[i, :, cols])
            acc[rows, cols] = part

    both(second, 0, "wait_recv")
    both(second_pass, 0, "start")
    both(second, 2, "start")
    ring_step(1)
    both(second, 1, "wait_recv")
    both(second_pass, 1, "start")
    both(second, 3, "start")
    project(0)
    ring_step(2)
    both(second, 2, "wait_recv")
    both(second_pass, 2, "start")
    project(1)
    ring_step(3)
    both(second, 3, "wait_recv")
    both(second_pass, 3, "start")
    project(2)
    project(3)

    run[...] = jnp.zeros_like(run)

    def qkv(b, h, slot):
        return acc[pl.ds(pl.multiple_of(b * 128, 128), 128), slot * 256 + h * 128:slot * 256 + (h + 1) * 128]

    @pl.loop(0, 6)
    def _(b):
        for h in range(2):
            keys = qkv(b, h, 1).astype(BF).astype(F32)
            decayed = (keys * rem[b, h]).astype(BF)
            own = lax.dot_general(decayed, qkv(b, h, 2).astype(BF), tn, preferred_element_type=F32)
            bsv[b, h] = own
            run[h] = cend[b, h, 0:1, :] * run[h] + own

    s_s[...] = run[...].astype(BF)
    s_copy = rc(s_s, s_r, ss.at[0], ss.at[1], sibling)
    s_copy.start()

    def in_block(b):
        for h in range(2):
            scores = lax.dot_general(
                qkv(b, h, 0).astype(BF), qkv(b, h, 1).astype(BF), nt, preferred_element_type=F32
            )
            scores = (scores * wgt[b, h]).astype(BF)
            within[pl.ds(pl.multiple_of(b * 128, 128), 128), h * 128:(h + 1) * 128] = dot(
                scores, qkv(b, h, 2).astype(BF)
            )

    @pl.loop(0, 2)
    def _(b):
        in_block(b)

    d_share.wait_recv()
    s_copy.wait_recv()
    mine_s, their_s = run[c], s_r[c].astype(F32)
    low = c == 0
    s0 = jnp.where(low, mine_s, their_s)
    s1 = jnp.where(low, their_s, mine_s)
    hc = pl.ds(c, 1)
    d1 = jnp.where(low, d_s[0, hc, :], d_o[0, hc, :])
    c_s[...] = (jnp.exp(d1) * s0 + s1).astype(BF)

    def c_copy(d):
        return rc(c_s, c_r.at[d - 1], cs_s.at[d - 1], cs_r.at[d - 1], at_z(d))

    for d in (4, 3, 5, 2, 6, 1, 7):
        c_copy(d).start()

    @pl.loop(2, 6)
    def _(b):
        in_block(b)

    @pl.loop(0, 6)
    def _(b):
        rows = pl.ds(pl.multiple_of(b * 128, 128), 128)
        gate = acc[rows, 768:1024]
        acc[rows, 768:1024] = gate / (1.0 + jnp.exp(-gate)) * gain[...]

    ring_step(4)
    for d in range(1, NZ):
        c_copy(d).wait_recv()
    enter = jnp.zeros((128, 128), F32)
    for d in range(NZ - 1, 0, -1):
        chip = jnp.exp(d_o[d, hc, :] + d_s[d, hc, :])
        enter = jnp.where(z >= d, chip * enter + c_r[d - 1].astype(F32), enter)
    i_s[...] = enter
    i_copy = rc(i_s, i_r, is_s.at[0], is_s.at[1], sibling)
    i_copy.start()
    i_copy.wait_recv()
    for h in range(2):
        base = jnp.where(c == h, i_s[...], i_r[...])
        inc[h] = jnp.where(
            c == 1, jnp.exp(d_s[0, h:h + 1, :]) * base + s_r[h].astype(F32), base
        )

    @pl.loop(0, 6)
    def _(b):
        rows = pl.ds(pl.multiple_of(b * 128, 128), 128)
        for h in range(2):
            state = inc[h]
            cols = slice(h * 128, (h + 1) * 128)
            carried = dot(qkv(b, h, 0).astype(BF), state.astype(BF)) * ecum[b, h]
            att = within[rows, cols] + carried
            scale = lax.rsqrt(jnp.mean(att * att, axis=1, keepdims=True) + EPSILON)
            gated2[rows, cols] = (att * scale * acc[rows, 768 + h * 128:768 + (h + 1) * 128]).astype(BF)
            inc[h] = cend[b, h, 0:1, :] * state + bsv[b, h]

    gated[...] = gated2[...].reshape(4, 4, 48, 256)

    def a_copy(kind, d):
        if kind == 0:
            src, dev = gated.at[lax.rem(x + d, 4)], at_x(d)
        else:
            src, dev = gated.at[:, lax.rem(y + d, 4)], at_y(d)
        j = kind * 3 + 3 - d
        return rc(src, ha.at[j], as_s.at[j], as_r.at[j], dev)

    for d in (2, 1, 3):
        a_copy(0, d).start()
        a_copy(1, d).start()
    wo_in.wait()
    for n in range(8):
        share_wait(n)
    for d in (1, 2, 3):
        a_copy(0, d).wait_recv()
        a_copy(1, d).wait_recv()

    def r_copy(n, kind, d):
        i = kind * 4 + n
        spot = lax.rem((y if kind == 0 else x) + d, 4)
        return rc(
            ps.at[i, spot], pr.at[i, 3 - d], rs_s.at[i, 3 - d], rs_r.at[i, 3 - d],
            at_y(d) if kind == 0 else at_x(d),
        )

    @pl.loop(0, 4)
    def _(n):
        for kind in (0, 1):
            cols = pl.ds(pl.multiple_of(n * CW, CW), CW)
            ocols = pl.ds(pl.multiple_of(kind * 2048 + n * CW, CW), CW)
            own = (gated[x] if kind == 0 else gated[:, y]).reshape(192, 256)
            part = dot(own, wo[:, ocols])
            for j in range(3):
                part += dot(ha[kind * 3 + j].reshape(192, 256), wg[kind * 3 + j, :, cols])
            ps[kind * 4 + n] = part.astype(BF).reshape(4, 48, CW)
            for d in (2, 1, 3):
                r_copy(n, kind, d).start()

    @pl.loop(0, 4)
    def _(n):
        for kind in (0, 1):
            i = kind * 4 + n
            for d in (1, 2, 3):
                r_copy(n, kind, d).wait_recv()
            total = ps[i, y if kind == 0 else x].astype(F32)
            for j in range(3):
                total += pr[i, j].astype(F32)
            out[:, pl.ds(pl.multiple_of(kind * 2048 + n * CW, CW), CW)] = total

    tail.wait_send()
    for d in range(1, NZ):
        d_copy(d).wait_send()
        c_copy(d).wait_send()
    d_share.wait_send()
    s_copy.wait_send()
    i_copy.wait_send()
    for kind in (0, 1):
        for d in (1, 2, 3):
            w0(kind, d).wait_send()
            a_copy(kind, d).wait_send()
    for k in (1, 2, 3, 4):
        ring(k, True).wait_send()
        ring(k, False).wait_send()
    for n in range(8):
        share(n).wait_send()

    @pl.loop(0, 4)
    def _(p):
        for make in (first, first_pass, second, second_pass):
            both(make, p, "wait_send")
        for kind in (0, 1):
            for d in (1, 2, 3):
                r_copy(p, kind, d).wait_send()


def main_call(fine, w, wo, gain, decay):
    vm = pltpu.VMEM
    dma = pltpu.SemaphoreType.DMA
    anyspace = pl.BlockSpec(memory_space=pl.ANY)
    vmem = pl.BlockSpec(memory_space=pltpu.VMEM)
    return pl.pallas_call(
        main_kernel,
        out_shape=jax.ShapeDtypeStruct((48, 4096), F32),
        in_specs=[anyspace, anyspace, anyspace, vmem, vmem],
        out_specs=vmem,
        scratch_shapes=[
            vm((NC, 192, CW), BF), vm((4 * NC, 200, 128), F32), vm((NC, 8, CW), BF), vm((NC, 8, CW), BF),
            vm((NC, 4, 4, 48, CW), BF), vm((2, CW * 8, 128), BF), vm((CW * 8, 128), F32),
            vm((NC, CW, 1024), BF), vm((768, 1024), F32), vm((6, 256, 2048), BF), vm((256, 4096), BF),
            vm((768, 256), BF), vm((4, 4, 48, 256), BF), vm((6, 4, 48, 256), BF),
            vm((8, 4, 48, CW), BF), vm((8, 3, 48, CW), BF),
            vm((6, 2, 128, 128), F32), vm((6, 2, 128, 128), F32), vm((6, 2, 128, 128), F32),
            vm((6, 2, 8, 128), F32), vm((6, 2, 128, 128), F32), vm((2, 128, 128), F32),
            vm((2, 128, 128), BF), vm((2, 128, 128), BF), vm((128, 128), BF), vm((7, 128, 128), BF),
            vm((128, 128), F32), vm((128, 128), F32), vm((2, 128, 128), F32), vm((768, 256), F32),
            vm((8, 8, 128), F32), vm((8, 8, 128), F32),
            dma((NC,)), dma((2,)), dma,
            dma((2,)), dma((NC, 4)), dma((NC, 4)), dma((NC, 4)), dma((NC, 4)), dma((6,)), dma((6,)),
            dma((8,)), dma((8,)), dma((8,)), dma((8,)),
            dma((7,)), dma((7,)), dma((2,)), dma((2,)), dma((7,)), dma((7,)), dma((2,)),
            dma((6,)), dma((6,)), dma((8, 3)), dma((8, 3)),
        ],
        compiler_params=pltpu.CompilerParams(
            collective_id=0, has_side_effects=True, vmem_limit_bytes=62 * 1024 * 1024
        ),
        name="coarse_level",
    )(fine, w, wo, gain, decay)


def add_kernel(fine, coarse, out, up):
    for q in range(fine.shape[1] // 128):
        cols = slice(q * 128, (q + 1) * 128)
        for m in range(4):
            up[q, pl.ds(m, 48, stride=4), :] = coarse[:, cols]
        out[:, cols] = (fine[:, cols].astype(F32) + up[q]).astype(BF)


def add_call(fine, coarse):
    wide = 1024
    return pl.pallas_call(
        add_kernel,
        grid=(4096 // wide,),
        out_shape=jax.ShapeDtypeStruct((192, 4096), BF),
        in_specs=[pl.BlockSpec((192, wide), lambda i: (0, i)), pl.BlockSpec((48, wide), lambda i: (0, i))],
        out_specs=pl.BlockSpec((192, wide), lambda i: (0, i)),
        scratch_shapes=[pltpu.VMEM((wide // 128, 192, 128), F32)],
        name="upsample_add",
    )(fine, coarse)


def body(fine_rows, w_inputs, w_out, head_gain, decay_log):
    w = w_inputs.reshape(4096, 4, 2, 128).transpose(0, 2, 1, 3).reshape(32768, 128)
    coarse = main_call(fine_rows, w, w_out, head_gain.reshape(1, 256), decay_log)
    return add_call(fine_rows, coarse)


def solution(mesh):
    return jax.shard_map(
        body,
        mesh=mesh,
        in_specs=(
            P(("seq", "mp"), None),
            P(None, None, "mp"),
            P("mp", None),
            P("mp"),
            P("mp", "seq"),
        ),
        out_specs=P(("seq", "mp"), None),
        check_vma=False,
    )
```

```python
import jax
import jax.numpy as jnp
from jax import lax
from jax.experimental import pallas as pl
from jax.experimental.pallas import tpu as pltpu
from jax.sharding import PartitionSpec as P

BF = jnp.bfloat16
F32 = jnp.float32
MESH = pl.DeviceIdType.MESH
EPSILON = 1e-05
CW = 512
NC = 8
NZ = 8


def dot(a, b):
    return jnp.dot(a, b, preferred_element_type=F32)


def main_kernel(
    fine, w, wo_hbm, gain, decay, out,
    fine_v, rows_f, tail_s, tail_r, g, w_raw, w_f, w_v, acc, wg, wo,
    gated2, gated, ha, ps, pr, ph,
    wgt, ecum, rem, cend, bsv, run, s_s, s_r, c_s, c_r, i_s, i_r, inc, within, d_o, d_s,
    l_fine, l_w, l_wo,
    tail_sem, p1s, p1r, p2s, p2r, w0s, w0r, rgs, rgr, sbs, sbr,
    dds, ddr, dss, ss, cs_s, cs_r, is_s, as_s, as_r, rs_s, rs_r, hs, hr,
):
    sq, mp = lax.axis_index("seq"), lax.axis_index("mp")
    z, c = lax.div(sq, 2), lax.rem(sq, 2)
    x, y = lax.div(mp, 4), lax.rem(mp, 4)
    flat = sq * 16 + mp

    def at_x(d):
        return (sq, lax.rem(x + d, 4) * 4 + y)

    def at_y(d):
        return (sq, x * 4 + lax.rem(y + d, 4))

    def at_z(d):
        return (lax.rem(z + d, NZ) * 2 + c, mp)

    sibling = (z * 2 + 1 - c, mp)
    after, before = lax.rem(flat + 1, 256), lax.rem(flat + 255, 256)
    after = (lax.div(after, 16), lax.rem(after, 16))
    before = (lax.div(before, 16), lax.rem(before, 16))

    def rc(src, dst, send, recv, dev):
        return pltpu.make_async_remote_copy(
            src_ref=src, dst_ref=dst, send_sem=send, recv_sem=recv,
            device_id=dev, device_id_type=MESH,
        )

    barrier = pltpu.get_barrier_semaphore()
    partners = (
        [at_x(1), at_x(3), at_y(1), at_y(3), at_z(1), at_z(NZ - 1), sibling, after, before]
    )
    for dev in partners:
        pl.semaphore_signal(barrier, inc=1, device_id=dev, device_id_type=MESH)

    fine_in = [
        pltpu.make_async_copy(fine.at[:, i * CW:(i + 1) * CW], fine_v.at[i], l_fine.at[i])
        for i in range(NC)
    ]
    for copy in fine_in:
        copy.start()

    def w_in(i, slot):
        return pltpu.make_async_copy(
            w.at[pl.ds(pl.multiple_of(i * CW * 8, CW * 8), CW * 8), :], w_raw.at[slot], l_w.at[slot]
        )

    w_in(0, 0).start()
    w_in(1, 1).start()
    wo_in = pltpu.make_async_copy(wo_hbm, wo, l_wo)
    wo_in.start()

    for copy in fine_in:
        copy.wait()

    def pool_into(i, first, count):
        for q in range(4):
            total = rows_f[4 * i + q, pl.ds(5 + 4 * first, count, stride=4), :]
            for m in (1, 2, 3):
                total += rows_f[4 * i + q, pl.ds(5 + 4 * first + m, count, stride=4), :]
            g[i, x, y, first:first + count, q * 128:(q + 1) * 128] = (total * 0.25).astype(BF)

    @pl.loop(0, NC)
    def _(i):
        for q in range(4):
            k = 4 * i + q
            rows_f[k, 8:200, :] = fine_v[i, :, q * 128:(q + 1) * 128].astype(F32)
            rows_f[k, 0:8, :] = jnp.zeros((8, 128), F32)
            tail_s[pl.ds(k, 1), :] = (
                rows_f[k, 197:198, :] + rows_f[k, 198:199, :] + rows_f[k, 199:200, :]
            )
        pool_into(i, 16, 32)

    total = jnp.sum(decay[...], axis=1, keepdims=True)
    d_o[0] = jnp.zeros((8, 128), F32)
    d_o[0, 0:2, :] = jnp.broadcast_to(total, (2, 128))

    pl.semaphore_wait(barrier, len(partners))

    tail = rc(tail_s, tail_r, tail_sem.at[0], tail_sem.at[1], after)
    tail.start()

    def d_step(k, right):
        src, dst = (k - 1, k) if right else ((NZ - k + 1) % NZ, NZ - k)
        return rc(d_o.at[src], d_o.at[dst], dds.at[dst - 1], ddr.at[dst - 1], at_z(1 if right else NZ - 1))

    def d_start(k):
        d_step(k, True).start()
        if k < 4:
            d_step(k, False).start()

    def d_wait(k):
        d_step(k, True).wait_recv()
        if k < 4:
            d_step(k, False).wait_recv()

    d_start(1)
    mine = pl.ds(pl.multiple_of(sq * 16, 16), 16)

    def w0(kind, d):
        at = at_x if kind == 0 else at_y
        j = kind * 3 + 3 - d
        src = wo_hbm.at[mine, kind * 2048:(kind + 1) * 2048] if d != 2 else wg.at[kind * 3 + 2, mine, :]
        return rc(src, wg.at[j, mine, :], w0s.at[j], w0r.at[j], at(d if d != 2 else 1))

    def first(i, kind, d, low=False):
        block = g.at[i, x, y, pl.ds(0, 16), :] if low else g.at[i, x, y, pl.ds(16, 32), :]
        k = (0 if d == 1 else 1) + (4 if low else 0)
        return rc(block, block, p1s.at[i, k], p1r.at[i, k], (at_x if kind == 0 else at_y)(d))

    def first_low(i, kind, d):
        return first(i, kind, d, True)

    def first_pass(i, kind, d):
        cols = pl.ds(0, 256) if d == 1 else pl.ds(256, 256)
        from_x = lax.rem(x + (4 - d), 4) if kind == 0 else x
        from_y = y if kind == 0 else lax.rem(y + (4 - d), 4)
        block = g.at[i, from_x, from_y, :, cols]
        k = 2 if d == 1 else 3
        return rc(block, block, p1s.at[i, k], p1r.at[i, k], (at_x if kind == 0 else at_y)(d))

    def second(i, kind, d):
        block = g.at[i, :, y] if kind == 0 else g.at[i, x]
        k = 0 if d == 1 else 1
        return rc(block, block, p2s.at[i, k], p2r.at[i, k], (at_y if kind == 0 else at_x)(d))

    def second_pass(i, kind, d):
        cols = pl.ds(0, 256) if d == 1 else pl.ds(256, 256)
        if kind == 0:
            block = g.at[i, :, lax.rem(y + (4 - d), 4), :, cols]
        else:
            block = g.at[i, lax.rem(x + (4 - d), 4), :, :, cols]
        k = 2 if d == 1 else 3
        return rc(block, block, p2s.at[i, k], p2r.at[i, k], (at_y if kind == 0 else at_x)(d))

    def both(make, p, act):
        for kind in (0, 1):
            for d in (1, 3):
                getattr(make(2 * p + kind, kind, d), act)()

    @pl.loop(0, 4)
    def _(p):
        both(first, p, "start")

    for d in (1, 3):
        w0(0, d).start()
        w0(1, d).start()
    acc[...] = jnp.zeros_like(acc)
    tail.wait_recv()
    is_first = flat == 0

    @pl.loop(0, 4)
    def _(p):
        for kind in (0, 1):
            i = 2 * p + kind
            for q in range(4):
                k = 4 * i + q
                rows_f[k, 7:8, :] = jnp.where(is_first, 0.0, tail_r[pl.ds(k, 1), :])
            pool_into(i, 0, 16)
        both(first_low, p, "start")

    def relayout(i, slot):
        w_in(i, slot).wait()
        w_f[...] = w_raw[slot].astype(F32)
        for s in range(4):
            for h in range(2):
                w_v[i, :, s * 256 + h * 128:s * 256 + (h + 1) * 128] = w_f[
                    pl.ds(h * 4 + s, CW, stride=8), :
                ].astype(BF)

        @pl.when(i + 2 < NC)
        def _():
            w_in(i + 2, slot).start()

    def rows_of(zz, cc):
        return pl.ds(pl.multiple_of((lax.rem(zz, NZ) * 2 + cc) * 16, 16), 16)

    def ring(k, right):
        which = slice(0, 6) if k < 4 else (slice(0, 3) if right else slice(3, 6))
        rows = rows_of(z + (NZ - (k - 1)) if right else z + (k - 1), c)
        block = wg.at[which, rows, :]
        n = 2 * (k - 1) + (0 if right else 1)
        return rc(block, block, rgs.at[n], rgr.at[n], at_z(1 if right else NZ - 1))

    def share(n):
        zz = z + (0, NZ - 1, NZ - 2, NZ - 3, 1, 2, 3, 4)[n]
        block = wg.at[:, rows_of(zz, c), :]
        return rc(block, block, sbs.at[n], sbr.at[n], sibling)

    def share_wait(n):
        zz = z + (0, NZ - 1, NZ - 2, NZ - 3, 1, 2, 3, 4)[n]
        block = wg.at[:, rows_of(zz, 1 - c), :]
        rc(block, block, sbs.at[n], sbr.at[n], sibling).wait_recv()

    def ring_step(k):
        ring(k, True).wait_recv()
        ring(k, False).wait_recv()
        if k < 4:
            ring(k + 1, True).start()
            ring(k + 1, False).start()
            share(k).start()
            share(3 + k).start()
        else:
            share(7).start()

    for kind in (0, 1):
        w0(kind, 1).wait_recv()
        w0(kind, 2).start()
    d_wait(1)
    d_start(2)

    @pl.loop(0, 4)
    def _(p):
        relayout(2 * p, 0)
        both(first, p, "wait_recv")
        both(first_low, p, "wait_recv")
        both(first_pass, p, "start")

    for kind in (0, 1):
        for d in (3, 2):
            w0(kind, d).wait_recv()
    ring(1, True).start()
    ring(1, False).start()
    share(0).start()
    d_wait(2)
    d_start(3)

    @pl.loop(0, 4)
    def _(p):
        both(first_pass, p, "wait_recv")

        @pl.when(p < 2)
        def _():
            both(second, p, "start")

        relayout(2 * p + 1, 1)

    d_wait(3)
    d_start(4)

    d_share = rc(d_o, d_s, dss.at[0], dss.at[1], sibling)

    t_i = lax.broadcasted_iota(jnp.int32, (128, 128), 0)
    s_i = lax.broadcasted_iota(jnp.int32, (128, 128), 1)
    causal = t_i >= s_i
    lower = jnp.where(causal, 1.0, 0.0).astype(F32)
    nt = (((1,), (1,)), ((), ()))
    tn = (((0,), (0,)), ((), ()))
    for b in range(6):
        for h in range(2):
            rep = jnp.broadcast_to(decay[h:h + 1, b * 128:(b + 1) * 128], (128, 128))
            col = lax.dot_general(lower, rep, nt, precision=lax.Precision.HIGHEST, preferred_element_type=F32)
            row = lax.dot_general(rep, lower, nt, precision=lax.Precision.HIGHEST, preferred_element_type=F32)
            wgt[b, h] = jnp.where(causal, jnp.exp(jnp.minimum(col - row, 0.0)), 0.0)
            ecum[b, h] = jnp.exp(col)
            end = col[127:128, :]
            rem[b, h] = jnp.exp(end - col)
            cend[b, h] = jnp.broadcast_to(jnp.exp(end), (8, 128))

    def project(p, slots=(0, 1, 2, 3)):
        step = slots[1] - slots[0]

        @pl.loop(0, 2 * len(slots))
        def _(t):
            i2 = lax.rem(t, 2)
            n = slots[0] + step * lax.div(t, 2)
            rows = pl.ds(pl.multiple_of(i2 * 384, 384), 384)
            cols = pl.ds(pl.multiple_of(n * 256, 256), 256)
            part = acc[rows, cols]
            for kind in (0, 1):
                i = 2 * p + kind
                left = g[i, pl.ds(i2 * 2, 2)].reshape(384, CW)
                part += dot(left, w_v[i, :, cols])
            acc[rows, cols] = part

    both(second, 0, "wait_recv")
    both(second_pass, 0, "start")
    both(second, 2, "start")
    d_wait(4)
    d_share.start()
    both(second, 1, "wait_recv")
    both(second_pass, 1, "start")
    both(second, 3, "start")
    ring_step(1)
    both(second_pass, 0, "wait_recv")
    project(0)
    both(second, 2, "wait_recv")
    both(second_pass, 2, "start")
    both(second_pass, 1, "wait_recv")
    project(1)
    both(second, 3, "wait_recv")
    both(second_pass, 3, "start")
    ring_step(2)
    both(second_pass, 2, "wait_recv")
    project(2)
    both(second_pass, 3, "wait_recv")
    project(3, (1, 2))

    run[...] = jnp.zeros_like(run)

    def qkv(b, h, slot):
        return acc[pl.ds(pl.multiple_of(b * 128, 128), 128), slot * 256 + h * 128:slot * 256 + (h + 1) * 128]

    @pl.loop(0, 6)
    def _(b):
        for h in range(2):
            keys = qkv(b, h, 1).astype(BF).astype(F32)
            decayed = (keys * rem[b, h]).astype(BF)
            own = lax.dot_general(decayed, qkv(b, h, 2).astype(BF), tn, preferred_element_type=F32)
            bsv[b, h] = own
            run[h] = cend[b, h, 0:1, :] * run[h] + own

    s_s[...] = run[...].astype(BF)
    s_copy = rc(s_s, s_r, ss.at[0], ss.at[1], sibling)
    s_copy.start()

    def in_block(b):
        for h in range(2):
            scores = lax.dot_general(
                qkv(b, h, 0).astype(BF), qkv(b, h, 1).astype(BF), nt, preferred_element_type=F32
            )
            scores = (scores * wgt[b, h]).astype(BF)
            within[pl.ds(pl.multiple_of(b * 128, 128), 128), h * 128:(h + 1) * 128] = dot(
                scores, qkv(b, h, 2).astype(BF)
            )

    project(3, (0, 3))
    ring_step(3)
    d_share.wait_recv()
    s_copy.wait_recv()
    mine_s, their_s = run[c], s_r[c].astype(F32)
    low = c == 0
    s0 = jnp.where(low, mine_s, their_s)
    s1 = jnp.where(low, their_s, mine_s)
    hc = pl.ds(c, 1)
    d1 = jnp.where(low, d_s[0, hc, :], d_o[0, hc, :])
    c_s[...] = (jnp.exp(d1) * s0 + s1).astype(BF)

    def c_copy(d):
        return rc(c_s, c_r.at[d - 1], cs_s.at[d - 1], cs_r.at[d - 1], at_z(d))

    for d in (4, 3, 5, 2, 6, 1, 7):
        c_copy(d).start()

    @pl.loop(0, 6)
    def _(b):
        in_block(b)

    @pl.loop(0, 6)
    def _(b):
        rows = pl.ds(pl.multiple_of(b * 128, 128), 128)
        gate = acc[rows, 768:1024]
        acc[rows, 768:1024] = gate / (1.0 + jnp.exp(-gate)) * gain[...]

    ring_step(4)
    for d in range(1, NZ):
        c_copy(d).wait_recv()
    enter = jnp.zeros((128, 128), F32)
    for d in range(NZ - 1, 0, -1):
        chip = jnp.exp(d_o[d, hc, :] + d_s[d, hc, :])
        enter = jnp.where(z >= d, chip * enter + c_r[d - 1].astype(F32), enter)
    i_s[...] = enter
    i_copy = rc(i_s, i_r, is_s.at[0], is_s.at[1], sibling)
    i_copy.start()
    i_copy.wait_recv()
    for h in range(2):
        base = jnp.where(c == h, i_s[...], i_r[...])
        inc[h] = jnp.where(
            c == 1, jnp.exp(d_s[0, h:h + 1, :]) * base + s_r[h].astype(F32), base
        )

    @pl.loop(0, 6)
    def _(b):
        rows = pl.ds(pl.multiple_of(b * 128, 128), 128)
        for h in range(2):
            state = inc[h]
            cols = slice(h * 128, (h + 1) * 128)
            carried = dot(qkv(b, h, 0).astype(BF), state.astype(BF)) * ecum[b, h]
            att = within[rows, cols] + carried
            scale = lax.rsqrt(jnp.mean(att * att, axis=1, keepdims=True) + EPSILON)
            gated2[rows, cols] = (att * scale * acc[rows, 768 + h * 128:768 + (h + 1) * 128]).astype(BF)
            inc[h] = cend[b, h, 0:1, :] * state + bsv[b, h]

    gated[...] = gated2[...].reshape(4, 4, 48, 256)

    def a_copy(kind, d):
        if kind == 0:
            src, dev = gated.at[lax.rem(x + d, 4)], at_x(d)
        else:
            src, dev = gated.at[:, lax.rem(y + d, 4)], at_y(d)
        j = kind * 3 + 3 - d
        return rc(src, ha.at[j], as_s.at[j], as_r.at[j], dev)

    for d in (2, 1, 3):
        a_copy(0, d).start()
        a_copy(1, d).start()
    wo_in.wait()
    for n in range(8):
        share_wait(n)
    for d in (1, 2, 3):
        a_copy(0, d).wait_recv()
        a_copy(1, d).wait_recv()

    def spot(kind, d):
        return lax.rem((y if kind == 0 else x) + d, 4)

    def half(n, kind, d):
        i, k = kind * 4 + n, 0 if d == 1 else 1
        cols = pl.ds(k * 256, 256)
        return rc(
            ps.at[i, spot(kind, 2), :, cols], ph.at[i, k], hs.at[i, k], hr.at[i, k],
            (at_y if kind == 0 else at_x)(d),
        )

    def r_copy(n, kind, d):
        i, k = kind * 4 + n, 0 if d == 1 else 1
        return rc(
            ps.at[i, spot(kind, d)], pr.at[i, k], rs_s.at[i, k], rs_r.at[i, k],
            (at_y if kind == 0 else at_x)(d),
        )

    def pass_on(n):
        for kind in (0, 1):
            i = kind * 4 + n
            for k, d in ((0, 1), (1, 3)):
                half(n, kind, d).wait_recv()
                cols = slice(k * 256, (k + 1) * 256)
                to = spot(kind, d)
                ps[i, to, :, cols] = (ps[i, to, :, cols].astype(F32) + ph[i, k].astype(F32)).astype(BF)
                r_copy(n, kind, d).start()

    @pl.loop(0, 4)
    def _(n):
        for kind in (0, 1):
            cols = pl.ds(pl.multiple_of(n * CW, CW), CW)
            ocols = pl.ds(pl.multiple_of(kind * 2048 + n * CW, CW), CW)
            own = (gated[x] if kind == 0 else gated[:, y]).reshape(192, 256)
            part = dot(own, wo[:, ocols])
            for j in range(3):
                part += dot(ha[kind * 3 + j].reshape(192, 256), wg[kind * 3 + j, :, cols])
            ps[kind * 4 + n] = part.astype(BF).reshape(4, 48, CW)
            for d in (1, 3):
                half(n, kind, d).start()

        @pl.when(n > 0)
        def _():
            pass_on(n - 1)

    pass_on(3)

    def put(i):
        return pltpu.make_async_copy(
            fine_v.at[i], out.at[:, pl.ds(pl.multiple_of(i * CW, CW), CW)], l_fine.at[i]
        )

    @pl.loop(0, 4)
    def _(n):
        for kind in (0, 1):
            i = kind * 4 + n
            for d in (1, 3):
                r_copy(n, kind, d).wait_recv()
            own = spot(kind, 0)
            for q in range(4):
                cols = slice(q * 128, (q + 1) * 128)
                total = ps[i, own, :, cols].astype(F32)
                for k in (0, 1):
                    total += pr[i, k, :, cols].astype(F32)
                for m in range(4):
                    rows_f[4 * i + q, pl.ds(m, 48, stride=4), :] = total
                fine_v[i, :, cols] = (
                    fine_v[i, :, cols].astype(F32) + rows_f[4 * i + q, 0:192, :]
                ).astype(BF)
            put(i).start()

    tail.wait_send()
    for k in (1, 2, 3, 4):
        d_step(k, True).wait_send()
        if k < 4:
            d_step(k, False).wait_send()
        ring(k, True).wait_send()
        ring(k, False).wait_send()
    for d in range(1, NZ):
        c_copy(d).wait_send()
    d_share.wait_send()
    s_copy.wait_send()
    i_copy.wait_send()
    for kind in (0, 1):
        for d in (1, 2, 3):
            w0(kind, d).wait_send()
            a_copy(kind, d).wait_send()
    for n in range(8):
        share(n).wait_send()

    @pl.loop(0, 4)
    def _(p):
        for make in (first, first_low, first_pass, second, second_pass):
            both(make, p, "wait_send")
        for kind in (0, 1):
            for d in (1, 3):
                half(p, kind, d).wait_send()
                r_copy(p, kind, d).wait_send()
            put(2 * p + kind).wait()


def main_call(fine, w, wo, gain, decay):
    vm = pltpu.VMEM
    dma = pltpu.SemaphoreType.DMA
    anyspace = pl.BlockSpec(memory_space=pl.ANY)
    vmem = pl.BlockSpec(memory_space=pltpu.VMEM)
    return pl.pallas_call(
        main_kernel,
        out_shape=jax.ShapeDtypeStruct((192, 4096), BF),
        in_specs=[anyspace, anyspace, anyspace, vmem, vmem],
        out_specs=anyspace,
        scratch_shapes=[
            vm((NC, 192, CW), BF), vm((4 * NC, 200, 128), F32), vm((32, 128), F32), vm((32, 128), F32),
            vm((NC, 4, 4, 48, CW), BF), vm((2, CW * 8, 128), BF), vm((CW * 8, 128), F32),
            vm((NC, CW, 1024), BF), vm((768, 1024), F32), vm((6, 256, 2048), BF), vm((256, 4096), BF),
            vm((768, 256), BF), vm((4, 4, 48, 256), BF), vm((6, 4, 48, 256), BF),
            vm((8, 4, 48, CW), BF), vm((8, 2, 48, CW), BF), vm((8, 2, 48, 256), BF),
            vm((6, 2, 128, 128), F32), vm((6, 2, 128, 128), F32), vm((6, 2, 128, 128), F32),
            vm((6, 2, 8, 128), F32), vm((6, 2, 128, 128), F32), vm((2, 128, 128), F32),
            vm((2, 128, 128), BF), vm((2, 128, 128), BF), vm((128, 128), BF), vm((7, 128, 128), BF),
            vm((128, 128), F32), vm((128, 128), F32), vm((2, 128, 128), F32), vm((768, 256), F32),
            vm((8, 8, 128), F32), vm((8, 8, 128), F32),
            dma((NC,)), dma((2,)), dma,
            dma((2,)), dma((NC, 6)), dma((NC, 6)), dma((NC, 4)), dma((NC, 4)), dma((6,)), dma((6,)),
            dma((8,)), dma((8,)), dma((8,)), dma((8,)),
            dma((7,)), dma((7,)), dma((2,)), dma((2,)), dma((7,)), dma((7,)), dma((2,)),
            dma((6,)), dma((6,)), dma((8, 2)), dma((8, 2)), dma((8, 2)), dma((8, 2)),
        ],
        compiler_params=pltpu.CompilerParams(
            collective_id=0, has_side_effects=True, vmem_limit_bytes=62 * 1024 * 1024
        ),
        name="coarse_level",
    )(fine, w, wo, gain, decay)


def body(fine_rows, w_inputs, w_out, head_gain, decay_log):
    w = w_inputs.reshape(4096, 4, 2, 128).transpose(0, 2, 1, 3).reshape(32768, 128)
    return main_call(fine_rows, w, w_out, head_gain.reshape(1, 256), decay_log)


def solution(mesh):
    return jax.shard_map(
        body,
        mesh=mesh,
        in_specs=(
            P(("seq", "mp"), None),
            P(None, None, "mp"),
            P("mp", None),
            P("mp"),
            P("mp", "seq"),
        ),
        out_specs=P(("seq", "mp"), None),
        check_vma=False,
    )
```

```python
import jax
import jax.numpy as jnp
from jax import lax
from jax.experimental import pallas as pl
from jax.experimental.pallas import tpu as pltpu
from jax.sharding import PartitionSpec as P

BF = jnp.bfloat16
F32 = jnp.float32
MESH = pl.DeviceIdType.MESH
EPSILON = 1e-05
CW = 512
NC = 8
NZ = 8


def dot(a, b):
    return jnp.dot(a, b, preferred_element_type=F32)


def main_kernel(
    fine, w, wo_hbm, gain, decay, out,
    fine_v, rows_f, tail_s, tail_r, g, w_raw, w_f, w_v, acc, wg, wo,
    gated2, gated, ha, ps, pr, ph,
    wgt, ecum, rem, cend, bsv, run, s_s, s_r, c_s, c_r, i_s, i_r, inc, within, d_o, d_s, dec,
    l_fine, l_w, l_wo,
    tail_sem, p1s, p1r, p2s, p2r, w0s, w0r, rgs, rgr, sbs, sbr,
    dds, ddr, dss, ss, cs_s, cs_r, is_s, as_s, as_r, rs_s, rs_r, hs, hr,
):
    sq, mp = lax.axis_index("seq"), lax.axis_index("mp")
    z, c = lax.div(sq, 2), lax.rem(sq, 2)
    x, y = lax.div(mp, 4), lax.rem(mp, 4)
    flat = sq * 16 + mp

    def at_x(d):
        return (sq, lax.rem(x + d, 4) * 4 + y)

    def at_y(d):
        return (sq, x * 4 + lax.rem(y + d, 4))

    def at_z(d):
        return (lax.rem(z + d, NZ) * 2 + c, mp)

    sibling = (z * 2 + 1 - c, mp)

    def rc(src, dst, send, recv, dev):
        return pltpu.make_async_remote_copy(
            src_ref=src, dst_ref=dst, send_sem=send, recv_sem=recv,
            device_id=dev, device_id_type=MESH,
        )

    barrier = pltpu.get_barrier_semaphore()
    partners = (
        [at_x(1), at_x(3), at_y(1), at_y(3), at_z(1), at_z(NZ - 1), sibling]
    )
    for dev in partners:
        pl.semaphore_signal(barrier, inc=1, device_id=dev, device_id_type=MESH)

    fine_in = [
        pltpu.make_async_copy(fine.at[:, i * CW:(i + 1) * CW], fine_v.at[i], l_fine.at[i])
        for i in range(NC)
    ]
    for copy in fine_in:
        copy.start()

    def w_in(i, slot):
        return pltpu.make_async_copy(
            w.at[pl.ds(pl.multiple_of(i * CW * 8, CW * 8), CW * 8), :], w_raw.at[slot], l_w.at[slot]
        )

    w_in(0, 0).start()
    w_in(1, 1).start()
    wo_in = pltpu.make_async_copy(wo_hbm, wo, l_wo)
    wo_in.start()

    for copy in fine_in:
        copy.wait()

    def pool_into(i, first, count):
        for q in range(4):
            total = rows_f[4 * i + q, pl.ds(5 + 4 * first, count, stride=4), :]
            for m in (1, 2, 3):
                total += rows_f[4 * i + q, pl.ds(5 + 4 * first + m, count, stride=4), :]
            g[i, x, y, first:first + count, q * 128:(q + 1) * 128] = (total * 0.25).astype(BF)

    @pl.loop(0, NC)
    def _(i):
        for q in range(4):
            k = 4 * i + q
            rows_f[k, 8:200, :] = fine_v[i, :, q * 128:(q + 1) * 128].astype(F32)
            rows_f[k, 0:8, :] = jnp.zeros((8, 128), F32)
            tail_s[pl.ds(k, 1), :] = (
                rows_f[k, 197:198, :] + rows_f[k, 198:199, :] + rows_f[k, 199:200, :]
            )
        pool_into(i, 16, 32)

    total = jnp.sum(decay[...], axis=1, keepdims=True)
    d_o[0] = jnp.zeros((8, 128), F32)
    d_o[0, 0:2, :] = jnp.broadcast_to(total, (2, 128))

    t_i = lax.broadcasted_iota(jnp.int32, (128, 128), 0)
    s_i = lax.broadcasted_iota(jnp.int32, (128, 128), 1)
    causal = t_i >= s_i
    lower = jnp.where(causal, 1.0, 0.0).astype(F32)
    nt = (((1,), (1,)), ((), ()))
    tn = (((0,), (0,)), ((), ()))
    dec[...] = jnp.zeros_like(dec)
    for b in range(6):
        for h in range(2):
            dec[2 * b + h:2 * b + h + 1, :] = decay[h:h + 1, b * 128:(b + 1) * 128]
    exact = dict(precision=lax.Precision.HIGHEST, preferred_element_type=F32)
    down = lax.dot_general(lower, dec[...], nt, **exact)
    across = lax.dot_general(dec[...], lower, nt, **exact)
    for b in range(6):
        for h in range(2):
            k = 2 * b + h
            col = jnp.broadcast_to(down[:, k:k + 1], (128, 128))
            row = across[k:k + 1, :]
            wgt[b, h] = jnp.where(causal, jnp.exp(jnp.minimum(col - row, 0.0)), 0.0)
            ecum[b, h] = jnp.exp(col)
            end = col[127:128, :]
            rem[b, h] = jnp.exp(end - col)
            cend[b, h] = jnp.broadcast_to(jnp.exp(end), (8, 128))

    pl.semaphore_wait(barrier, len(partners))

    tails = [
        rc(src, dst, tail_sem.at[2 * n], tail_sem.at[2 * n + 1], dev)
        for n, (src, dst, dev) in enumerate((
            (tail_s, tail_r.at[0], at_y(1)),
            (tail_r.at[0], tail_r.at[1], at_x(1)),
            (tail_r.at[1], tail_r.at[2], sibling),
            (tail_r.at[1], tail_r.at[3], at_z(1)),
            (tail_r.at[3], tail_r.at[2], sibling),
        ))
    ]
    tails[0].start()

    def d_step(k, right):
        src, dst = (k - 1, k) if right else ((NZ - k + 1) % NZ, NZ - k)
        return rc(d_o.at[src], d_o.at[dst], dds.at[dst - 1], ddr.at[dst - 1], at_z(1 if right else NZ - 1))

    def d_start(k):
        d_step(k, True).start()
        if k < 4:
            d_step(k, False).start()

    def d_wait(k):
        d_step(k, True).wait_recv()
        if k < 4:
            d_step(k, False).wait_recv()

    d_start(1)
    d_own = rc(d_o.at[0], d_s.at[0], dss.at[2], dss.at[3], sibling)
    d_own.start()
    d_share = rc(d_o.at[1:8], d_s.at[1:8], dss.at[0], dss.at[1], sibling)

    mine = pl.ds(pl.multiple_of(sq * 16, 16), 16)

    def w0(kind, d):
        at = at_x if kind == 0 else at_y
        j = kind * 3 + 3 - d
        src = wo_hbm.at[mine, kind * 2048:(kind + 1) * 2048] if d != 2 else wg.at[kind * 3 + 2, mine, :]
        return rc(src, wg.at[j, mine, :], w0s.at[j], w0r.at[j], at(d if d != 2 else 1))

    def part_of(low):
        return (pl.ds(0, 16), 1) if low else (pl.ds(16, 32), 0)

    def first(p, kind, d, low):
        i, (rows, lo) = 2 * p + kind, part_of(low)
        block = g.at[i, x, y, rows, :]
        return rc(block, block, p1s.at[i], p1r.at[p, 0, lo], (at_x if kind == 0 else at_y)(d))

    def first_pass(p, kind, d, low):
        i, (rows, lo) = 2 * p + kind, part_of(low)
        cols = pl.ds(0, 256) if d == 1 else pl.ds(256, 256)
        from_x = lax.rem(x + (4 - d), 4) if kind == 0 else x
        from_y = y if kind == 0 else lax.rem(y + (4 - d), 4)
        block = g.at[i, from_x, from_y, rows, cols]
        return rc(block, block, p1s.at[i], p1r.at[p, 1, lo], (at_x if kind == 0 else at_y)(d))

    def second(p, kind, d, low):
        i, (rows, lo) = 2 * p + kind, part_of(low)
        block = g.at[i, :, y, rows, :] if kind == 0 else g.at[i, x, :, rows, :]
        return rc(block, block, p2s.at[i], p2r.at[p, 0, lo], (at_y if kind == 0 else at_x)(d))

    def second_pass(p, kind, d, low):
        i, (rows, lo) = 2 * p + kind, part_of(low)
        cols = pl.ds(0, 256) if d == 1 else pl.ds(256, 256)
        if kind == 0:
            block = g.at[i, :, lax.rem(y + (4 - d), 4), rows, cols]
        else:
            block = g.at[i, lax.rem(x + (4 - d), 4), :, rows, cols]
        return rc(block, block, p2s.at[i], p2r.at[p, 1, lo], (at_y if kind == 0 else at_x)(d))

    def begin(make, p, low=False):
        for kind in (0, 1):
            for d in (1, 3):
                make(p, kind, d, low).start()

    def got(ref, sem):
        rc(ref, ref, ss.at[0], sem, sibling).wait_recv()

    def gone(ref, sem):
        rc(ref, ref, sem, ss.at[1], sibling).wait_send()

    def arrived(make, p, low=False):
        rows, lo = part_of(low)
        pair = pl.ds(2 * p, 2)
        if make is first:
            got(g.at[pair, 0, pl.ds(0, 2), rows, :], p1r.at[p, 0, lo])
        elif make is first_pass:
            got(g.at[pair, 0, 0, rows, :], p1r.at[p, 1, lo])
        elif make is second:
            got(g.at[pair, pl.ds(0, 2), :, rows, :], p2r.at[p, 0, lo])
        else:
            got(g.at[pair, 0, :, rows, :], p2r.at[p, 1, lo])

    def relayout(i):
        slot = i % 2
        w_in(i, slot).wait()
        w_f[...] = w_raw[slot].astype(F32)
        for s in range(4):
            for h in range(2):
                w_v[i, :, s * 256 + h * 128:s * 256 + (h + 1) * 128] = w_f[
                    pl.ds(h * 4 + s, CW, stride=8), :
                ].astype(BF)

        if i + 2 < NC:
            w_in(i + 2, slot).start()

    def rows_of(zz, cc):
        return pl.ds(pl.multiple_of((lax.rem(zz, NZ) * 2 + cc) * 16, 16), 16)

    def ring(k, right):
        which = slice(0, 6) if k < 4 else (slice(0, 3) if right else slice(3, 6))
        rows = rows_of(z + (NZ - (k - 1)) if right else z + (k - 1), c)
        block = wg.at[which, rows, :]
        n = 2 * (k - 1) + (0 if right else 1)
        return rc(block, block, rgs.at[n], rgr.at[n], at_z(1 if right else NZ - 1))

    def share(n):
        zz = z + (0, NZ - 1, NZ - 2, NZ - 3, 1, 2, 3, 4)[n]
        block = wg.at[:, rows_of(zz, c), :]
        return rc(block, block, sbs.at[n], sbr.at[n], sibling)

    def share_wait(n):
        zz = z + (0, NZ - 1, NZ - 2, NZ - 3, 1, 2, 3, 4)[n]
        block = wg.at[:, rows_of(zz, 1 - c), :]
        rc(block, block, sbs.at[n], sbr.at[n], sibling).wait_recv()

    def ring_step(k):
        if k != 3:
            d_wait(k)
        if k < 3:
            d_start(k + 1)
        elif k == 4:
            d_share.start()
        ring(k, True).wait_recv()
        ring(k, False).wait_recv()
        if k < 4:
            ring(k + 1, True).start()
            ring(k + 1, False).start()
            share(k).start()
            share(3 + k).start()
        else:
            share(7).start()

    @pl.loop(0, 4)
    def _(p):
        begin(first, p)

    for d in (1, 3):
        w0(0, d).start()
        w0(1, d).start()
    relayout(0)
    tails[0].wait_recv()

    @pl.when(y == 0)
    def _():
        tails[1].start()

    relayout(1)

    @pl.loop(0, 4)
    def _(p):
        arrived(first, p)
        begin(first_pass, p)

    for kind in (0, 1):
        w0(kind, 1).wait_recv()
        w0(kind, 2).start()

    @pl.loop(0, 3)
    def _(p):
        arrived(first_pass, p)
        begin(second, p)

    @pl.when(y == 0)
    def _():
        tails[1].wait_recv()

    @pl.when((mp == 0) & (c == 0))
    def _():
        tails[2].start()

    @pl.when((mp == 0) & (c == 1))
    def _():
        tails[3].start()

    for kind in (0, 1):
        for d in (3, 2):
            w0(kind, d).wait_recv()
    ring(1, True).start()
    ring(1, False).start()
    share(0).start()
    acc[...] = jnp.zeros_like(acc)
    relayout(2)
    relayout(3)

    arrived(first_pass, 3)
    relayout(4)

    @pl.when((mp == 0) & (c == 1))
    def _():
        tails[2].wait_recv()
        tails[3].wait_recv()
        tails[4].start()

    relayout(5)

    def project(p, low, slots=(0, 1, 2, 3)):
        step = slots[1] - slots[0]
        tall, off, xs = (16, 0, 4) if low else (32, 16, 2)

        @pl.loop(0, 4 // xs * len(slots))
        def _(t):
            i2 = lax.rem(t, 4 // xs)
            n = slots[0] + step * lax.div(t, 4 // xs)
            cols = pl.ds(pl.multiple_of(n * 256, 256), 256)
            part = jnp.zeros((256, 256), F32)
            for kind in (0, 1):
                i = 2 * p + kind
                left = g[i, pl.ds(i2 * xs, xs), :, off:off + tall, :].reshape(256, CW)
                part += dot(left, w_v[i, :, cols])
            for k in range(4 * xs):
                rows = pl.ds(pl.multiple_of(i2 * 384 + k * 48 + off, 16), tall)
                acc[rows, cols] += part[k * tall:(k + 1) * tall]

    def go_on(p, low):
        arrived(second, p, low)
        begin(second_pass, p, low)

    go_on(0, False)
    begin(second, 3)
    relayout(6)

    @pl.when((mp == 0) & (c == 0))
    def _():
        tails[4].wait_recv()

    is_first = flat == 0
    from_tail = jnp.where(y > 0, 0, jnp.where(x > 0, 1, 2))

    @pl.loop(0, 4)
    def _(p):
        for kind in (0, 1):
            i = 2 * p + kind
            for q in range(4):
                k = 4 * i + q
                rows_f[k, 7:8, :] = jnp.where(is_first, 0.0, tail_r[from_tail, pl.ds(k, 1), :])
            pool_into(i, 0, 16)
        begin(first, p, True)

    go_on(1, False)
    relayout(7)
    go_on(2, False)
    arrived(second_pass, 0)
    project(0, False)
    ring_step(1)
    go_on(3, False)

    @pl.loop(0, 4)
    def _(p):
        arrived(first, p, True)
        begin(first_pass, p, True)

    arrived(second_pass, 1)
    project(1, False)

    @pl.loop(0, 4)
    def _(p):
        arrived(first_pass, p, True)
        begin(second, p, True)

    arrived(second_pass, 2)
    project(2, False)
    arrived(second_pass, 3)
    go_on(0, True)
    project(3, False)
    go_on(1, True)
    ring_step(2)
    go_on(2, True)
    go_on(3, True)
    for p in (0, 1, 2):
        arrived(second_pass, p, True)
        project(p, True)
    arrived(second_pass, 3, True)
    project(3, True, (1, 2))

    run[...] = jnp.zeros_like(run)

    def qkv(b, h, slot):
        return acc[pl.ds(pl.multiple_of(b * 128, 128), 128), slot * 256 + h * 128:slot * 256 + (h + 1) * 128]

    @pl.loop(0, 6)
    def _(b):
        for h in range(2):
            keys = qkv(b, h, 1).astype(BF).astype(F32)
            decayed = (keys * rem[b, h]).astype(BF)
            own = lax.dot_general(decayed, qkv(b, h, 2).astype(BF), tn, preferred_element_type=F32)
            bsv[b, h] = own
            run[h] = cend[b, h, 0:1, :] * run[h] + own

    s_s[...] = run[...].astype(BF)
    s_copy = rc(s_s, s_r, ss.at[0], ss.at[1], sibling)
    s_copy.start()

    def in_block(b):
        for h in range(2):
            scores = lax.dot_general(
                qkv(b, h, 0).astype(BF), qkv(b, h, 1).astype(BF), nt, preferred_element_type=F32
            )
            scores = (scores * wgt[b, h]).astype(BF)
            within[pl.ds(pl.multiple_of(b * 128, 128), 128), h * 128:(h + 1) * 128] = dot(
                scores, qkv(b, h, 2).astype(BF)
            )

    project(3, True, (0, 3))
    d_own.wait_recv()
    s_copy.wait_recv()
    mine_s, their_s = run[c], s_r[c].astype(F32)
    low = c == 0
    s0 = jnp.where(low, mine_s, their_s)
    s1 = jnp.where(low, their_s, mine_s)
    hc = pl.ds(c, 1)
    d1 = jnp.where(low, d_s[0, hc, :], d_o[0, hc, :])
    c_s[...] = (jnp.exp(d1) * s0 + s1).astype(BF)

    def c_copy(d):
        return rc(c_s, c_r.at[d - 1], cs_s.at[d - 1], cs_r.at[d - 1], at_z(d))

    d_wait(3)
    d_start(4)
    for d in (4, 3, 5, 2, 6, 1, 7):
        c_copy(d).start()

    @pl.loop(0, 6)
    def _(b):
        in_block(b)

    @pl.loop(0, 6)
    def _(b):
        rows = pl.ds(pl.multiple_of(b * 128, 128), 128)
        gate = acc[rows, 768:1024]
        acc[rows, 768:1024] = gate / (1.0 + jnp.exp(-gate)) * gain[...]

    ring_step(3)
    for d in range(1, NZ):
        c_copy(d).wait_recv()
    ring_step(4)
    d_share.wait_recv()
    enter = jnp.zeros((128, 128), F32)
    for d in range(NZ - 1, 0, -1):
        chip = jnp.exp(d_o[d, hc, :] + d_s[d, hc, :])
        enter = jnp.where(z >= d, chip * enter + c_r[d - 1].astype(F32), enter)
    i_s[...] = enter
    i_copy = rc(i_s, i_r, is_s.at[0], is_s.at[1], sibling)
    i_copy.start()
    i_copy.wait_recv()
    for h in range(2):
        base = jnp.where(c == h, i_s[...], i_r[...])
        inc[h] = jnp.where(
            c == 1, jnp.exp(d_s[0, h:h + 1, :]) * base + s_r[h].astype(F32), base
        )

    @pl.loop(0, 6)
    def _(b):
        rows = pl.ds(pl.multiple_of(b * 128, 128), 128)
        for h in range(2):
            state = inc[h]
            cols = slice(h * 128, (h + 1) * 128)
            carried = dot(qkv(b, h, 0).astype(BF), state.astype(BF)) * ecum[b, h]
            att = within[rows, cols] + carried
            scale = lax.rsqrt(jnp.mean(att * att, axis=1, keepdims=True) + EPSILON)
            gated2[rows, cols] = (att * scale * acc[rows, 768 + h * 128:768 + (h + 1) * 128]).astype(BF)
            inc[h] = cend[b, h, 0:1, :] * state + bsv[b, h]

    gated[...] = gated2[...].reshape(4, 4, 48, 256)

    def piece(kind, d):
        return gated.at[lax.rem(x + d, 4)] if kind == 0 else gated.at[:, lax.rem(y + d, 4)]

    def a_copy(kind, d):
        j = kind * 3 + 3 - d
        return rc(piece(kind, d), ha.at[j], as_s.at[j], as_r.at[j], (at_x if kind == 0 else at_y)(d))

    for d in (2, 1, 3):
        a_copy(0, d).start()
        a_copy(1, d).start()
    wo_in.wait()
    for n in range(8):
        share_wait(n)
    for kind in (0, 1):
        for d in (1, 3, 2):
            a_copy(kind, d).wait_recv()

    def spot(kind, d):
        return lax.rem((y if kind == 0 else x) + d, 4)

    def half(n, kind, d):
        i, k = kind * 4 + n, 0 if d == 1 else 1
        cols = pl.ds(k * 256, 256)
        return rc(
            ps.at[i, spot(kind, 2), :, cols], ph.at[i, k], hs.at[i], hr.at[i],
            (at_y if kind == 0 else at_x)(d),
        )

    def r_copy(n, kind, d):
        i, k = kind * 4 + n, 0 if d == 1 else 1
        return rc(
            ps.at[i, spot(kind, d)], pr.at[i, k], rs_s.at[i], rs_r.at[i],
            (at_y if kind == 0 else at_x)(d),
        )

    def pass_on(n):
        for kind in (0, 1):
            i = kind * 4 + n
            got(ph.at[i], hr.at[i])
            for k, d in ((0, 1), (1, 3)):
                cols = slice(k * 256, (k + 1) * 256)
                to = spot(kind, d)
                ps[i, to, :, cols] = (ps[i, to, :, cols].astype(F32) + ph[i, k].astype(F32)).astype(BF)
                r_copy(n, kind, d).start()

    @pl.loop(0, 4)
    def _(n):
        for kind in (0, 1):
            cols = pl.ds(pl.multiple_of(n * CW, CW), CW)
            ocols = pl.ds(pl.multiple_of(kind * 2048 + n * CW, CW), CW)
            own = (gated[x] if kind == 0 else gated[:, y]).reshape(192, 256)
            part = dot(own, wo[:, ocols])
            for j in range(3):
                part += dot(ha[kind * 3 + j].reshape(192, 256), wg[kind * 3 + j, :, cols])
            ps[kind * 4 + n] = part.astype(BF).reshape(4, 48, CW)
            for d in (1, 3):
                half(n, kind, d).start()

        @pl.when(n > 1)
        def _():
            pass_on(n - 2)


    def put(i):
        return pltpu.make_async_copy(
            fine_v.at[i], out.at[:, pl.ds(pl.multiple_of(i * CW, CW), CW)], l_fine.at[i]
        )

    def finish(n):
        for kind in (0, 1):
            i = kind * 4 + n
            got(pr.at[i], rs_r.at[i])
            own = spot(kind, 0)
            for q in range(4):
                cols = slice(q * 128, (q + 1) * 128)
                total = ps[i, own, :, cols].astype(F32)
                for k in (0, 1):
                    total += pr[i, k, :, cols].astype(F32)
                for m in range(4):
                    rows_f[4 * i + q, pl.ds(m, 48, stride=4), :] = total
                fine_v[i, :, cols] = (
                    fine_v[i, :, cols].astype(F32) + rows_f[4 * i + q, 0:192, :]
                ).astype(BF)
            put(i).start()

    pass_on(2)
    pass_on(3)

    @pl.loop(0, 4)
    def _(n):
        finish(n)

    tails[0].wait_send()

    @pl.when(y == 0)
    def _():
        tails[1].wait_send()

    @pl.when((mp == 0) & (c == 0))
    def _():
        tails[2].wait_send()

    @pl.when((mp == 0) & (c == 1))
    def _():
        tails[3].wait_send()
        tails[4].wait_send()

    for k in (1, 2, 3, 4):
        d_step(k, True).wait_send()
        if k < 4:
            d_step(k, False).wait_send()
        ring(k, True).wait_send()
        ring(k, False).wait_send()
    for d in range(1, NZ):
        c_copy(d).wait_send()
    d_share.wait_send()
    d_own.wait_send()
    s_copy.wait_send()
    i_copy.wait_send()
    for kind in (0, 1):
        for d in (1, 2, 3):
            w0(kind, d).wait_send()
            a_copy(kind, d).wait_send()
    for n in range(8):
        share(n).wait_send()

    @pl.loop(0, 4)
    def _(p):
        for kind in (0, 1):
            i = 2 * p + kind
            gone(g.at[i, 0, pl.ds(0, 3)], p1s.at[i])
            gone(g.at[i, pl.ds(0, 3)], p2s.at[i])
            gone(ph.at[i], hs.at[i])
            gone(pr.at[i], rs_s.at[i])
            put(2 * p + kind).wait()


def main_call(fine, w, wo, gain, decay):
    vm = pltpu.VMEM
    dma = pltpu.SemaphoreType.DMA
    anyspace = pl.BlockSpec(memory_space=pl.ANY)
    vmem = pl.BlockSpec(memory_space=pltpu.VMEM)
    return pl.pallas_call(
        main_kernel,
        out_shape=jax.ShapeDtypeStruct((192, 4096), BF),
        in_specs=[anyspace, anyspace, anyspace, vmem, vmem],
        out_specs=anyspace,
        scratch_shapes=[
            vm((NC, 192, CW), BF), vm((4 * NC, 200, 128), F32), vm((32, 128), F32), vm((4, 32, 128), F32),
            vm((NC, 4, 4, 48, CW), BF), vm((2, CW * 8, 128), BF), vm((CW * 8, 128), F32),
            vm((NC, CW, 1024), BF), vm((768, 1024), F32), vm((6, 256, 2048), BF), vm((256, 4096), BF),
            vm((768, 256), BF), vm((4, 4, 48, 256), BF), vm((6, 4, 48, 256), BF),
            vm((8, 4, 48, CW), BF), vm((8, 2, 48, CW), BF), vm((8, 2, 48, 256), BF),
            vm((6, 2, 128, 128), F32), vm((6, 2, 128, 128), F32), vm((6, 2, 128, 128), F32),
            vm((6, 2, 8, 128), F32), vm((6, 2, 128, 128), F32), vm((2, 128, 128), F32),
            vm((2, 128, 128), BF), vm((2, 128, 128), BF), vm((128, 128), BF), vm((7, 128, 128), BF),
            vm((128, 128), F32), vm((128, 128), F32), vm((2, 128, 128), F32), vm((768, 256), F32),
            vm((8, 8, 128), F32), vm((8, 8, 128), F32), vm((128, 128), F32),
            dma((NC,)), dma((2,)), dma,
            dma((10,)), dma((NC,)), dma((4, 2, 2)), dma((NC,)), dma((4, 2, 2)), dma((6,)), dma((6,)),
            dma((8,)), dma((8,)), dma((8,)), dma((8,)),
            dma((7,)), dma((7,)), dma((4,)), dma((2,)), dma((7,)), dma((7,)), dma((2,)),
            dma((6,)), dma((6,)), dma((8,)), dma((8,)), dma((8,)), dma((8,)),
        ],
        compiler_params=pltpu.CompilerParams(
            collective_id=0, has_side_effects=True, vmem_limit_bytes=62 * 1024 * 1024
        ),
        name="coarse_level",
    )(fine, w, wo, gain, decay)


def body(fine_rows, w_inputs, w_out, head_gain, decay_log):
    w = w_inputs.reshape(4096, 4, 2, 128).transpose(0, 2, 1, 3).reshape(32768, 128)
    return main_call(fine_rows, w, w_out, head_gain.reshape(1, 256), decay_log)


def solution(mesh):
    return jax.shard_map(
        body,
        mesh=mesh,
        in_specs=(
            P(("seq", "mp"), None),
            P(None, None, "mp"),
            P("mp", None),
            P("mp"),
            P("mp", "seq"),
        ),
        out_specs=P(("seq", "mp"), None),
        check_vma=False,
    )
```

```python
import jax
import jax.numpy as jnp
from jax import lax
from jax.experimental import pallas as pl
from jax.experimental.pallas import tpu as pltpu
from jax.sharding import PartitionSpec as P

BF = jnp.bfloat16
F32 = jnp.float32
MESH = pl.DeviceIdType.MESH
EPSILON = 1e-05
CW = 512
NC = 8
NZ = 8


def dot(a, b):
    return jnp.dot(a, b, preferred_element_type=F32)


def main_kernel(
    fine, w, wo_hbm, gain, decay, out,
    fine_v, rows_f, tail_s, tail_r, g, w_raw, w_f, w_v, acc, wg, wo,
    gated2, gated, ha, ps, pr, ph,
    wgt, ecum, rem, cend, bsv, run, s_s, s_r, c_s, c_r, i_s, i_r, inc, within, d_o, d_s, dec,
    l_fine, l_w, l_wo,
    tail_sem, p1s, p1r, p2s, p2r, w0s, w0r, rgs, rgr, sbs, sbr,
    dds, ddr, dss, ss, cs_s, cs_r, is_s, as_s, as_r, rs_s, rs_r, hs, hr,
):
    sq, mp = lax.axis_index("seq"), lax.axis_index("mp")
    z, c = lax.div(sq, 2), lax.rem(sq, 2)
    x, y = lax.div(mp, 4), lax.rem(mp, 4)
    flat = sq * 16 + mp

    def at_x(d):
        return (sq, lax.rem(x + d, 4) * 4 + y)

    def at_y(d):
        return (sq, x * 4 + lax.rem(y + d, 4))

    def at_z(d):
        return (lax.rem(z + d, NZ) * 2 + c, mp)

    sibling = (z * 2 + 1 - c, mp)

    def rc(src, dst, send, recv, dev):
        return pltpu.make_async_remote_copy(
            src_ref=src, dst_ref=dst, send_sem=send, recv_sem=recv,
            device_id=dev, device_id_type=MESH,
        )

    barrier = pltpu.get_barrier_semaphore()
    partners = (
        [at_x(1), at_x(3), at_y(1), at_y(3), at_z(1), at_z(NZ - 1), sibling]
    )
    for dev in partners:
        pl.semaphore_signal(barrier, inc=1, device_id=dev, device_id_type=MESH)

    fine_in = [
        pltpu.make_async_copy(fine.at[:, i * CW:(i + 1) * CW], fine_v.at[i], l_fine.at[i])
        for i in range(NC)
    ]
    for copy in fine_in:
        copy.start()

    def w_in(i, slot):
        return pltpu.make_async_copy(
            w.at[pl.ds(pl.multiple_of(i * CW * 8, CW * 8), CW * 8), :], w_raw.at[slot], l_w.at[slot]
        )

    w_in(0, 0).start()
    w_in(1, 1).start()
    wo_in = pltpu.make_async_copy(wo_hbm, wo, l_wo)
    wo_in.start()

    for copy in fine_in:
        copy.wait()

    def pool_into(i, first, count):
        for q in range(4):
            total = rows_f[4 * i + q, pl.ds(5 + 4 * first, count, stride=4), :]
            for m in (1, 2, 3):
                total += rows_f[4 * i + q, pl.ds(5 + 4 * first + m, count, stride=4), :]
            g[i, x, y, first:first + count, q * 128:(q + 1) * 128] = (total * 0.25).astype(BF)

    @pl.loop(0, NC)
    def _(i):
        for q in range(4):
            k = 4 * i + q
            rows_f[k, 8:200, :] = fine_v[i, :, q * 128:(q + 1) * 128].astype(F32)
            rows_f[k, 0:8, :] = jnp.zeros((8, 128), F32)
            tail_s[pl.ds(k, 1), :] = (
                rows_f[k, 197:198, :] + rows_f[k, 198:199, :] + rows_f[k, 199:200, :]
            )
        pool_into(i, 16, 32)

    total = jnp.sum(decay[...], axis=1, keepdims=True)
    d_o[0] = jnp.zeros((8, 128), F32)
    d_o[0, 0:2, :] = jnp.broadcast_to(total, (2, 128))

    t_i = lax.broadcasted_iota(jnp.int32, (128, 128), 0)
    s_i = lax.broadcasted_iota(jnp.int32, (128, 128), 1)
    causal = t_i >= s_i
    lower = jnp.where(causal, 1.0, 0.0).astype(F32)
    nt = (((1,), (1,)), ((), ()))
    tn = (((0,), (0,)), ((), ()))
    dec[...] = jnp.zeros_like(dec)
    for b in range(6):
        for h in range(2):
            dec[2 * b + h:2 * b + h + 1, :] = decay[h:h + 1, b * 128:(b + 1) * 128]
    exact = dict(precision=lax.Precision.HIGHEST, preferred_element_type=F32)
    down = lax.dot_general(lower, dec[...], nt, **exact)
    across = lax.dot_general(dec[...], lower, nt, **exact)
    for b in range(6):
        for h in range(2):
            k = 2 * b + h
            col = jnp.broadcast_to(down[:, k:k + 1], (128, 128))
            row = across[k:k + 1, :]
            wgt[b, h] = jnp.where(causal, jnp.exp(jnp.minimum(col - row, 0.0)), 0.0)
            ecum[b, h] = jnp.exp(col)
            end = col[127:128, :]
            rem[b, h] = jnp.exp(end - col)
            cend[b, h] = jnp.broadcast_to(jnp.exp(end), (8, 128))

    pl.semaphore_wait(barrier, len(partners))

    tails = [
        rc(src, dst, tail_sem.at[2 * n], tail_sem.at[2 * n + 1], dev)
        for n, (src, dst, dev) in enumerate((
            (tail_s, tail_r.at[0], at_y(1)),
            (tail_r.at[0], tail_r.at[1], at_x(1)),
            (tail_r.at[1], tail_r.at[2], sibling),
            (tail_r.at[1], tail_r.at[3], at_z(1)),
            (tail_r.at[3], tail_r.at[2], sibling),
        ))
    ]
    tails[0].start()

    def d_step(k, right):
        src, dst = (k - 1, k) if right else ((NZ - k + 1) % NZ, NZ - k)
        return rc(d_o.at[src], d_o.at[dst], dds.at[dst - 1], ddr.at[dst - 1], at_z(1 if right else NZ - 1))

    def d_start(k):
        d_step(k, True).start()
        if k < 4:
            d_step(k, False).start()

    def d_wait(k):
        d_step(k, True).wait_recv()
        if k < 4:
            d_step(k, False).wait_recv()

    d_start(1)
    d_own = rc(d_o.at[0], d_s.at[0], dss.at[2], dss.at[3], sibling)
    d_own.start()
    d_share = rc(d_o.at[1:8], d_s.at[1:8], dss.at[0], dss.at[1], sibling)

    mine = pl.ds(pl.multiple_of(sq * 16, 16), 16)

    def w0(kind, d):
        at = at_x if kind == 0 else at_y
        j = kind * 3 + 3 - d
        src = wo_hbm.at[mine, kind * 2048:(kind + 1) * 2048] if d != 2 else wg.at[kind * 3 + 2, mine, :]
        return rc(src, wg.at[j, mine, :], w0s.at[j], w0r.at[j], at(d if d != 2 else 1))

    def part_of(low):
        return (pl.ds(0, 16), 1) if low else (pl.ds(16, 32), 0)

    def first(p, kind, d, low):
        i, (rows, lo) = 2 * p + kind, part_of(low)
        block = g.at[i, x, y, rows, :]
        return rc(block, block, p1s.at[i], p1r.at[p, 0, lo], (at_x if kind == 0 else at_y)(d))

    def first_pass(p, kind, d, low):
        i, (rows, lo) = 2 * p + kind, part_of(low)
        cols = pl.ds(0, 256) if d == 1 else pl.ds(256, 256)
        from_x = lax.rem(x + (4 - d), 4) if kind == 0 else x
        from_y = y if kind == 0 else lax.rem(y + (4 - d), 4)
        block = g.at[i, from_x, from_y, rows, cols]
        return rc(block, block, p1s.at[i], p1r.at[p, 1, lo], (at_x if kind == 0 else at_y)(d))

    def second(p, kind, d, low):
        i, (rows, lo) = 2 * p + kind, part_of(low)
        block = g.at[i, :, y, rows, :] if kind == 0 else g.at[i, x, :, rows, :]
        return rc(block, block, p2s.at[i], p2r.at[p, 0, lo], (at_y if kind == 0 else at_x)(d))

    def second_pass(p, kind, d, low):
        i, (rows, lo) = 2 * p + kind, part_of(low)
        cols = pl.ds(0, 256) if d == 1 else pl.ds(256, 256)
        if kind == 0:
            block = g.at[i, :, lax.rem(y + (4 - d), 4), rows, cols]
        else:
            block = g.at[i, lax.rem(x + (4 - d), 4), :, rows, cols]
        return rc(block, block, p2s.at[i], p2r.at[p, 1, lo], (at_y if kind == 0 else at_x)(d))

    def begin(make, p, low=False):
        for kind in (0, 1):
            for d in (1, 3):
                make(p, kind, d, low).start()

    def got(ref, sem):
        rc(ref, ref, ss.at[0], sem, sibling).wait_recv()

    def gone(ref, sem):
        rc(ref, ref, sem, ss.at[1], sibling).wait_send()

    def arrived(make, p, low=False):
        rows, lo = part_of(low)
        pair = pl.ds(2 * p, 2)
        if make is first:
            got(g.at[pair, 0, pl.ds(0, 2), rows, :], p1r.at[p, 0, lo])
        elif make is first_pass:
            got(g.at[pair, 0, 0, rows, :], p1r.at[p, 1, lo])
        elif make is second:
            got(g.at[pair, pl.ds(0, 2), :, rows, :], p2r.at[p, 0, lo])
        else:
            got(g.at[pair, 0, :, rows, :], p2r.at[p, 1, lo])

    def relayout(i):
        slot = i % 2
        w_in(i, slot).wait()
        w_f[...] = w_raw[slot].astype(F32)
        for s in range(4):
            for h in range(2):
                w_v[i, :, s * 256 + h * 128:s * 256 + (h + 1) * 128] = w_f[
                    pl.ds(h * 4 + s, CW, stride=8), :
                ].astype(BF)

        if i + 2 < NC:
            w_in(i + 2, slot).start()

    def rows_of(zz, cc):
        return pl.ds(pl.multiple_of((lax.rem(zz, NZ) * 2 + cc) * 16, 16), 16)

    def ring(k, right):
        which = slice(0, 6) if k < 4 else (slice(0, 3) if right else slice(3, 6))
        rows = rows_of(z + (NZ - (k - 1)) if right else z + (k - 1), c)
        block = wg.at[which, rows, :]
        n = 2 * (k - 1) + (0 if right else 1)
        return rc(block, block, rgs.at[n], rgr.at[n], at_z(1 if right else NZ - 1))

    def share(n):
        zz = z + (0, NZ - 1, NZ - 2, NZ - 3, 1, 2, 3, 4)[n]
        block = wg.at[:, rows_of(zz, c), :]
        return rc(block, block, sbs.at[n], sbr.at[n], sibling)

    def share_wait(n):
        zz = z + (0, NZ - 1, NZ - 2, NZ - 3, 1, 2, 3, 4)[n]
        block = wg.at[:, rows_of(zz, 1 - c), :]
        rc(block, block, sbs.at[n], sbr.at[n], sibling).wait_recv()

    def ring_step(k):
        if k < 3:
            d_wait(k)
            d_start(k + 1)
        ring(k, True).wait_recv()
        ring(k, False).wait_recv()
        if k < 4:
            ring(k + 1, True).start()
            ring(k + 1, False).start()
            share(k).start()
            share(3 + k).start()
        else:
            share(7).start()

    @pl.loop(0, 4)
    def _(p):
        begin(first, p)

    for d in (1, 3):
        w0(0, d).start()
        w0(1, d).start()
    relayout(0)
    tails[0].wait_recv()

    @pl.when(y == 0)
    def _():
        tails[1].start()

    relayout(1)

    @pl.loop(0, 4)
    def _(p):
        arrived(first, p)
        begin(first_pass, p)

    for kind in (0, 1):
        w0(kind, 1).wait_recv()
        w0(kind, 2).start()

    @pl.loop(0, 3)
    def _(p):
        arrived(first_pass, p)
        begin(second, p)

    @pl.when(y == 0)
    def _():
        tails[1].wait_recv()

    @pl.when((mp == 0) & (c == 0))
    def _():
        tails[2].start()

    @pl.when((mp == 0) & (c == 1))
    def _():
        tails[3].start()

    for kind in (0, 1):
        for d in (3, 2):
            w0(kind, d).wait_recv()
    ring(1, True).start()
    ring(1, False).start()
    share(0).start()
    acc[...] = jnp.zeros_like(acc)
    relayout(2)
    relayout(3)

    arrived(first_pass, 3)
    relayout(4)

    @pl.when((mp == 0) & (c == 1))
    def _():
        tails[2].wait_recv()
        tails[3].wait_recv()
        tails[4].start()

    relayout(5)

    def project(p, low, slots=(0, 1, 2, 3)):
        step = slots[1] - slots[0]
        tall, off, xs = (16, 0, 4) if low else (32, 16, 2)

        @pl.loop(0, 4 // xs * len(slots))
        def _(t):
            i2 = lax.rem(t, 4 // xs)
            n = slots[0] + step * lax.div(t, 4 // xs)
            cols = pl.ds(pl.multiple_of(n * 256, 256), 256)
            part = jnp.zeros((256, 256), F32)
            for kind in (0, 1):
                i = 2 * p + kind
                left = g[i, pl.ds(i2 * xs, xs), :, off:off + tall, :].reshape(256, CW)
                part += dot(left, w_v[i, :, cols])
            for k in range(4 * xs):
                rows = pl.ds(pl.multiple_of(i2 * 384 + k * 48 + off, 16), tall)
                acc[rows, cols] += part[k * tall:(k + 1) * tall]

    def go_on(p, low):
        arrived(second, p, low)
        begin(second_pass, p, low)

    go_on(0, False)
    begin(second, 3)
    relayout(6)

    @pl.when((mp == 0) & (c == 0))
    def _():
        tails[4].wait_recv()

    is_first = flat == 0
    from_tail = jnp.where(y > 0, 0, jnp.where(x > 0, 1, 2))

    @pl.loop(0, 4)
    def _(p):
        for kind in (0, 1):
            i = 2 * p + kind
            for q in range(4):
                k = 4 * i + q
                rows_f[k, 7:8, :] = jnp.where(is_first, 0.0, tail_r[from_tail, pl.ds(k, 1), :])
            pool_into(i, 0, 16)
        begin(first, p, True)

    go_on(1, False)
    relayout(7)
    go_on(2, False)
    arrived(second_pass, 0)
    project(0, False)
    ring_step(1)
    go_on(3, False)

    @pl.loop(0, 4)
    def _(p):
        arrived(first, p, True)
        begin(first_pass, p, True)

    arrived(second_pass, 1)
    project(1, False)

    @pl.loop(0, 4)
    def _(p):
        arrived(first_pass, p, True)
        begin(second, p, True)

    arrived(second_pass, 2)
    project(2, False)
    arrived(second_pass, 3)
    go_on(0, True)
    project(3, False)
    go_on(1, True)
    ring_step(2)
    go_on(2, True)
    go_on(3, True)
    for p in (0, 1, 2):
        arrived(second_pass, p, True)
        project(p, True)
    arrived(second_pass, 3, True)
    project(3, True, (1, 2))

    run[...] = jnp.zeros_like(run)

    def qkv(b, h, slot):
        return acc[pl.ds(pl.multiple_of(b * 128, 128), 128), slot * 256 + h * 128:slot * 256 + (h + 1) * 128]

    @pl.loop(0, 6)
    def _(b):
        for h in range(2):
            keys = qkv(b, h, 1).astype(BF).astype(F32)
            decayed = (keys * rem[b, h]).astype(BF)
            own = lax.dot_general(decayed, qkv(b, h, 2).astype(BF), tn, preferred_element_type=F32)
            bsv[b, h] = own
            run[h] = cend[b, h, 0:1, :] * run[h] + own

    s_s[...] = run[...].astype(BF)
    s_copy = rc(s_s, s_r, ss.at[0], ss.at[1], sibling)
    s_copy.start()

    def in_block(b):
        for h in range(2):
            scores = lax.dot_general(
                qkv(b, h, 0).astype(BF), qkv(b, h, 1).astype(BF), nt, preferred_element_type=F32
            )
            scores = (scores * wgt[b, h]).astype(BF)
            within[pl.ds(pl.multiple_of(b * 128, 128), 128), h * 128:(h + 1) * 128] = dot(
                scores, qkv(b, h, 2).astype(BF)
            )

    project(3, True, (0, 3))
    d_own.wait_recv()
    s_copy.wait_recv()
    mine_s, their_s = run[c], s_r[c].astype(F32)
    low = c == 0
    s0 = jnp.where(low, mine_s, their_s)
    s1 = jnp.where(low, their_s, mine_s)
    hc = pl.ds(c, 1)
    d1 = jnp.where(low, d_s[0, hc, :], d_o[0, hc, :])
    c_s[...] = (jnp.exp(d1) * s0 + s1).astype(BF)

    def c_copy(d):
        return rc(c_s, c_r.at[d - 1], cs_s.at[d - 1], cs_r.at[d - 1], at_z(d))

    d_wait(3)
    d_start(4)
    for d in (4, 3, 5, 2, 6, 1, 7):
        c_copy(d).start()

    @pl.loop(0, 6)
    def _(b):
        in_block(b)

    @pl.loop(0, 6)
    def _(b):
        rows = pl.ds(pl.multiple_of(b * 128, 128), 128)
        gate = acc[rows, 768:1024]
        acc[rows, 768:1024] = gate / (1.0 + jnp.exp(-gate)) * gain[...]

    ring_step(3)
    d_wait(4)
    d_share.start()
    for d in range(1, NZ):
        c_copy(d).wait_recv()
    d_share.wait_recv()
    enter = jnp.zeros((128, 128), F32)
    for d in range(NZ - 1, 0, -1):
        chip = jnp.exp(d_o[d, hc, :] + d_s[d, hc, :])
        enter = jnp.where(z >= d, chip * enter + c_r[d - 1].astype(F32), enter)
    i_s[...] = enter
    i_copy = rc(i_s, i_r, is_s.at[0], is_s.at[1], sibling)
    i_copy.start()
    i_copy.wait_recv()
    for h in range(2):
        base = jnp.where(c == h, i_s[...], i_r[...])
        inc[h] = jnp.where(
            c == 1, jnp.exp(d_s[0, h:h + 1, :]) * base + s_r[h].astype(F32), base
        )

    @pl.loop(0, 6)
    def _(b):
        rows = pl.ds(pl.multiple_of(b * 128, 128), 128)
        for h in range(2):
            state = inc[h]
            cols = slice(h * 128, (h + 1) * 128)
            carried = dot(qkv(b, h, 0).astype(BF), state.astype(BF)) * ecum[b, h]
            att = within[rows, cols] + carried
            scale = lax.rsqrt(jnp.mean(att * att, axis=1, keepdims=True) + EPSILON)
            gated2[rows, cols] = (att * scale * acc[rows, 768 + h * 128:768 + (h + 1) * 128]).astype(BF)
            inc[h] = cend[b, h, 0:1, :] * state + bsv[b, h]

    gated[...] = gated2[...].reshape(4, 4, 48, 256)

    def piece(kind, d):
        return gated.at[lax.rem(x + d, 4)] if kind == 0 else gated.at[:, lax.rem(y + d, 4)]

    def a_copy(kind, d):
        j = kind * 3 + 3 - d
        return rc(piece(kind, d), ha.at[j], as_s.at[j], as_r.at[j], (at_x if kind == 0 else at_y)(d))

    for d in (2, 1, 3):
        a_copy(0, d).start()
        a_copy(1, d).start()
    wo_in.wait()
    ring_step(4)

    @pl.loop(0, 4)
    def _(n):
        for kind in (0, 1):
            ocols = pl.ds(pl.multiple_of(kind * 2048 + n * CW, CW), CW)
            own = (gated[x] if kind == 0 else gated[:, y]).reshape(192, 256)
            acc[pl.ds(pl.multiple_of(n * 192, 192), 192), kind * CW:(kind + 1) * CW] = dot(own, wo[:, ocols])

    for n in range(8):
        share_wait(n)
    for kind in (0, 1):
        for d in (1, 3, 2):
            a_copy(kind, d).wait_recv()

    def spot(kind, d):
        return lax.rem((y if kind == 0 else x) + d, 4)

    def half(n, kind, d):
        i, k = kind * 4 + n, 0 if d == 1 else 1
        cols = pl.ds(k * 256, 256)
        return rc(
            ps.at[i, spot(kind, 2), :, cols], ph.at[i, k], hs.at[i], hr.at[i],
            (at_y if kind == 0 else at_x)(d),
        )

    def r_copy(n, kind, d):
        i, k = kind * 4 + n, 0 if d == 1 else 1
        return rc(
            ps.at[i, spot(kind, d)], pr.at[i, k], rs_s.at[i], rs_r.at[i],
            (at_y if kind == 0 else at_x)(d),
        )

    def pass_on(n):
        for kind in (0, 1):
            i = kind * 4 + n
            got(ph.at[i], hr.at[i])
            for k, d in ((0, 1), (1, 3)):
                cols = slice(k * 256, (k + 1) * 256)
                to = spot(kind, d)
                ps[i, to, :, cols] = (ps[i, to, :, cols].astype(F32) + ph[i, k].astype(F32)).astype(BF)
                r_copy(n, kind, d).start()

    @pl.loop(0, 4)
    def _(n):
        for kind in (0, 1):
            cols = pl.ds(pl.multiple_of(n * CW, CW), CW)
            part = acc[pl.ds(pl.multiple_of(n * 192, 192), 192), kind * CW:(kind + 1) * CW]
            for j in range(3):
                part += dot(ha[kind * 3 + j].reshape(192, 256), wg[kind * 3 + j, :, cols])
            ps[kind * 4 + n] = part.astype(BF).reshape(4, 48, CW)
            for d in (1, 3):
                half(n, kind, d).start()

        @pl.when(n > 1)
        def _():
            pass_on(n - 2)


    def put(i):
        return pltpu.make_async_copy(
            fine_v.at[i], out.at[:, pl.ds(pl.multiple_of(i * CW, CW), CW)], l_fine.at[i]
        )

    def finish(n):
        for kind in (0, 1):
            i = kind * 4 + n
            got(pr.at[i], rs_r.at[i])
            own = spot(kind, 0)
            for q in range(4):
                cols = slice(q * 128, (q + 1) * 128)
                total = ps[i, own, :, cols].astype(F32)
                for k in (0, 1):
                    total += pr[i, k, :, cols].astype(F32)
                for m in range(4):
                    rows_f[4 * i + q, pl.ds(m, 48, stride=4), :] = total
                fine_v[i, :, cols] = (
                    fine_v[i, :, cols].astype(F32) + rows_f[4 * i + q, 0:192, :]
                ).astype(BF)
            put(i).start()

    pass_on(2)
    pass_on(3)

    @pl.loop(0, 4)
    def _(n):
        finish(n)

    tails[0].wait_send()

    @pl.when(y == 0)
    def _():
        tails[1].wait_send()

    @pl.when((mp == 0) & (c == 0))
    def _():
        tails[2].wait_send()

    @pl.when((mp == 0) & (c == 1))
    def _():
        tails[3].wait_send()
        tails[4].wait_send()

    for k in (1, 2, 3, 4):
        d_step(k, True).wait_send()
        if k < 4:
            d_step(k, False).wait_send()
        ring(k, True).wait_send()
        ring(k, False).wait_send()
    for d in range(1, NZ):
        c_copy(d).wait_send()
    d_share.wait_send()
    d_own.wait_send()
    s_copy.wait_send()
    i_copy.wait_send()
    for kind in (0, 1):
        for d in (1, 2, 3):
            w0(kind, d).wait_send()
            a_copy(kind, d).wait_send()
    for n in range(8):
        share(n).wait_send()

    @pl.loop(0, 4)
    def _(p):
        for kind in (0, 1):
            i = 2 * p + kind
            gone(g.at[i, 0, pl.ds(0, 3)], p1s.at[i])
            gone(g.at[i, pl.ds(0, 3)], p2s.at[i])
            gone(ph.at[i], hs.at[i])
            gone(pr.at[i], rs_s.at[i])
            put(2 * p + kind).wait()


def main_call(fine, w, wo, gain, decay):
    vm = pltpu.VMEM
    dma = pltpu.SemaphoreType.DMA
    anyspace = pl.BlockSpec(memory_space=pl.ANY)
    vmem = pl.BlockSpec(memory_space=pltpu.VMEM)
    return pl.pallas_call(
        main_kernel,
        out_shape=jax.ShapeDtypeStruct((192, 4096), BF),
        in_specs=[anyspace, anyspace, anyspace, vmem, vmem],
        out_specs=anyspace,
        scratch_shapes=[
            vm((NC, 192, CW), BF), vm((4 * NC, 200, 128), F32), vm((32, 128), F32), vm((4, 32, 128), F32),
            vm((NC, 4, 4, 48, CW), BF), vm((2, CW * 8, 128), BF), vm((CW * 8, 128), F32),
            vm((NC, CW, 1024), BF), vm((768, 1024), F32), vm((6, 256, 2048), BF), vm((256, 4096), BF),
            vm((768, 256), BF), vm((4, 4, 48, 256), BF), vm((6, 4, 48, 256), BF),
            vm((8, 4, 48, CW), BF), vm((8, 2, 48, CW), BF), vm((8, 2, 48, 256), BF),
            vm((6, 2, 128, 128), F32), vm((6, 2, 128, 128), F32), vm((6, 2, 128, 128), F32),
            vm((6, 2, 8, 128), F32), vm((6, 2, 128, 128), F32), vm((2, 128, 128), F32),
            vm((2, 128, 128), BF), vm((2, 128, 128), BF), vm((128, 128), BF), vm((7, 128, 128), BF),
            vm((128, 128), F32), vm((128, 128), F32), vm((2, 128, 128), F32), vm((768, 256), F32),
            vm((8, 8, 128), F32), vm((8, 8, 128), F32), vm((128, 128), F32),
            dma((NC,)), dma((2,)), dma,
            dma((10,)), dma((NC,)), dma((4, 2, 2)), dma((NC,)), dma((4, 2, 2)), dma((6,)), dma((6,)),
            dma((8,)), dma((8,)), dma((8,)), dma((8,)),
            dma((7,)), dma((7,)), dma((4,)), dma((2,)), dma((7,)), dma((7,)), dma((2,)),
            dma((6,)), dma((6,)), dma((8,)), dma((8,)), dma((8,)), dma((8,)),
        ],
        compiler_params=pltpu.CompilerParams(
            collective_id=0, has_side_effects=True, vmem_limit_bytes=62 * 1024 * 1024
        ),
        name="coarse_level",
    )(fine, w, wo, gain, decay)


def body(fine_rows, w_inputs, w_out, head_gain, decay_log):
    w = w_inputs.reshape(4096, 4, 2, 128).transpose(0, 2, 1, 3).reshape(32768, 128)
    return main_call(fine_rows, w, w_out, head_gain.reshape(1, 256), decay_log)


def solution(mesh):
    return jax.shard_map(
        body,
        mesh=mesh,
        in_specs=(
            P(("seq", "mp"), None),
            P(None, None, "mp"),
            P("mp", None),
            P("mp"),
            P("mp", "seq"),
        ),
        out_specs=P(("seq", "mp"), None),
        check_vma=False,
    )
```
